128 devices in a mesh: dp: 2 (over core), ctx: 16 (over z, y), head: 4 (over x).
Axes of the slice: x: 4, y: 4, z: 4, core: 2. Of those that a mesh axis runs over, the one named last changes fastest.
Arguments:
- queries: float32 [2, 4096, 64, 128], P('dp', 'ctx', 'head'), may hold values from -8 to 8
- key_rows: float32 [2, 4096, 8, 128], P('dp', 'ctx', 'head'), may hold values from -8 to 8
- value_rows: float32 [2, 4096, 8, 128], P('dp', 'ctx', 'head'), may hold values from -18 to 18
- query_map: float32 [64, 128, 128], P('head'), may hold values from -0.5 to 0.5
- key_map: float32 [8, 128, 128], P('head'), may hold values from -0.5 to 0.5
- block_doc: int32 [2, 16], P('dp'), may hold values from 0 to 4, never falling along the last dimension, each value on 1 to 9 neighbouring positions
Outputs:
- grad_queries: float32 [2, 4096, 64, 128], P('dp', 'ctx', 'head')
- grad_keys: float32 [2, 4096, 8, 128], P('dp', 'ctx', 'head')
- grad_values: float32 [2, 4096, 8, 128], P('dp', 'ctx', 'head')
- grad_query_map: float32 [64, 128, 128], P('head')
- grad_key_map: float32 [8, 128, 128], P('head')
The draws below stay inside these ranges and needn't reach their ends.
Inputs may be any that keep to these rules, and one draw needn't show every extreme that they name: `block_doc`: the document numbers of a sequence's blocks never fall along the sequence; each document covers 1 to 9 blocks in a row, and some document covers exactly 9.
All inputs are finite; a program needn't handle non-finite values.
Results may differ from the reference program's by a relative error of at most 0.0003.
Values sent between devices are 32-bit elements; how exact they have to be, the bound alone decides.
No kernel may reach another device: no remote copies, remote signals or barrier semaphores. Data moves between devices by JAX's collectives and lax.ppermute only.
A program may use at most 128 MiB of HBM per device.

```python
import math
import jax
import jax.numpy as jnp
import numpy as np
from jax import lax

D = 128
F = 128
KV_HEADS = 8
GROUP = 8
TOK_DEV = 256
QH = 64
LENGTH = 4096
SEQS = 2
MOST_BLOCKS = 9
DOCS = 5
N_CTX = 16


def draw_queries(key, part):
    own_key = jax.random.fold_in(key, 11)
    values = jnp.clip(jax.random.normal(own_key, (SEQS, LENGTH, QH, D), jnp.float32), -6.0, 6.0)
    return values


def draw_key_rows(key, part):
    own_key = jax.random.fold_in(key, 13)
    values = jnp.clip(jax.random.normal(own_key, (SEQS, LENGTH, KV_HEADS, D), jnp.float32), -6.0, 6.0)
    return values


def draw_value_rows(key, part):
    own_key = jax.random.fold_in(key, 17)
    head_pos = jnp.arange(KV_HEADS, dtype=jnp.float32) / (KV_HEADS - 1)
    rising = jnp.exp(math.log(3.0) * head_pos)
    values = jnp.clip(jax.random.normal(own_key, (SEQS, LENGTH, KV_HEADS, D), jnp.float32), -6.0, 6.0)
    return values * rising[None, None, :, None]


def map_draw(own_key, key, shape):
    values = jnp.clip(jax.random.normal(own_key, shape, jnp.float32) * D ** (-0.5), -0.5, 0.5)
    return values


def draw_query_map(key, part):
    return map_draw(jax.random.fold_in(key, 19), key, (QH, D, F))


def draw_key_map(key, part):
    return map_draw(jax.random.fold_in(key, 23), key, (KV_HEADS, D, F))


def profile(count, total, bound, lean):
    loads = [(1 << 20) // math.isqrt(standing ** lean) + 1 for standing in range(2, count + 1)]
    spare, holding = total - bound - (count - 1), [1] * (count - 1)
    while spare > 0:
        free = [i for i in range(count - 1) if holding[i] < bound]
        whole, budget = sum([loads[i] for i in free]), spare
        for i in free:
            addition = min(bound - holding[i], max(1, budget * loads[i] // whole), spare)
            holding[i] = holding[i] + addition
            spare = spare - addition
    return np.array([bound] + holding)


def uneven(key, count, total, reach, lean):
    if count == 2:
        one = jax.random.randint(key, (), max(1, total - reach), min(reach, total - 1) + 1)
        return jnp.stack([one, total - one])
    tallies = jnp.asarray(profile(count, total, reach, lean), jnp.int32)
    couples = (count - 1) // 2
    giver, receiver = tallies[1:1 + 2 * couples:2], tallies[2:2 + 2 * couples:2]
    margin = jnp.minimum(giver - 1, reach - receiver)
    shifted = jax.random.randint(jax.random.fold_in(key, 1), (couples,), 0, 1 << 20) % (margin + 1)
    tallies = tallies.at[1:1 + 2 * couples:2].set(giver - shifted).at[2:2 + 2 * couples:2].set(receiver + shifted)
    return tallies[jax.random.permutation(jax.random.fold_in(key, 2), count)]


def setup_inputs(seed: int = 0) -> dict:
    streams_of = jax.random.split(jax.random.key(seed), 7)
    queries = draw_queries(jax.random.fold_in(streams_of[6], 71), 0)
    key_rows = draw_key_rows(jax.random.fold_in(streams_of[6], 71), 0)
    value_rows = draw_value_rows(jax.random.fold_in(streams_of[6], 71), 0)
    query_map = draw_query_map(jax.random.fold_in(streams_of[6], 71), 0)
    key_map = draw_key_map(jax.random.fold_in(streams_of[6], 71), 0)
    block_doc = jax.vmap(lambda own: jnp.searchsorted(jnp.cumsum(uneven(own, DOCS, N_CTX, MOST_BLOCKS, 0)), jnp.arange(N_CTX), side="right"))(jax.random.split(streams_of[5], SEQS)).reshape((SEQS, N_CTX)).astype(jnp.int32)
    return dict(queries=queries, key_rows=key_rows, value_rows=value_rows, query_map=query_map, key_map=key_map, block_doc=block_doc)


exact_math = lax.Precision.HIGHEST

def feature_map(inputs, weights):
    return jax.nn.softmax(jnp.dot(inputs, weights, precision=exact_math), axis=-1)

def teacher_head(query_rows, key_block, value_block, visible, score_scale):
    scores = jnp.dot(query_rows, key_block.T, precision=exact_math) * score_scale
    scores = jnp.where(visible, scores, -jnp.inf)
    return jnp.dot(jax.nn.softmax(scores, axis=-1), value_block, precision=exact_math)

def student_head(query_rows, key_block, value_block, query_weights, key_weights, mask_rows):
    query_feats = feature_map(query_rows, query_weights)
    key_feats = feature_map(key_block, key_weights)
    scores = jnp.dot(query_feats, key_feats.T, precision=exact_math) * mask_rows
    numerator = jnp.dot(scores, value_block, precision=exact_math)
    return numerator / lax.optimization_barrier(jnp.sum(scores, axis=-1))[:, None]

def reference(queries, key_rows, value_rows, query_map, key_map, block_doc):
    length = queries.shape[1]
    head_width = queries.shape[3]
    kv_count = key_rows.shape[2]
    score_scale = 1.0 / math.sqrt(head_width)
    positions = jnp.arange(length, dtype=jnp.int32)
    key_weights = jnp.repeat(key_map, GROUP, axis=0)
    query_grads = []
    key_grads = []
    value_grads = []
    map_query_sum = jnp.zeros(query_map.shape, query_map.dtype)
    map_key_sum = jnp.zeros(key_weights.shape, key_map.dtype)
    for sequence in range(queries.shape[0]):
        doc_ids = block_doc[sequence][positions // TOK_DEV]
        visible = (positions[None, :] <= positions[:, None]) & (doc_ids[None, :] == doc_ids[:, None])
        mask_rows = visible.astype(queries.dtype)
        query_heads = jnp.transpose(queries[sequence], (1, 0, 2))
        key_heads = jnp.repeat(jnp.transpose(key_rows[sequence], (1, 0, 2)), GROUP, axis=0)
        value_heads = jnp.repeat(jnp.transpose(value_rows[sequence], (1, 0, 2)), GROUP, axis=0)

        def run_teacher(packed):
            return teacher_head(packed[0], packed[1], packed[2], visible, score_scale)
        teacher = lax.map(run_teacher, (query_heads, key_heads, value_heads))
        mean_square = lax.optimization_barrier(jnp.mean(teacher * teacher, axis=(0, 2))) + 1e-06

        def run_student(packed):

            def student_of(query_rows, key_block, value_block, query_weights, key_weight_one):
                return student_head(query_rows, key_block, value_block, query_weights, key_weight_one, mask_rows)
            student, pullback = jax.vjp(student_of, packed[0], packed[1], packed[2], packed[3], packed[4])
            return pullback(2.0 * (student - packed[5]) / mean_square[:, None])
        gradients = lax.map(run_student, (query_heads, key_heads, value_heads, query_map, key_weights, teacher))
        query_grads.append(jnp.transpose(gradients[0], (1, 0, 2)))
        key_sum = lax.optimization_barrier(jnp.sum(gradients[1].reshape(kv_count, GROUP, length, head_width), axis=1))
        value_sum = lax.optimization_barrier(jnp.sum(gradients[2].reshape(kv_count, GROUP, length, head_width), axis=1))
        key_grads.append(jnp.transpose(key_sum, (1, 0, 2)))
        value_grads.append(jnp.transpose(value_sum, (1, 0, 2)))
        map_query_sum = map_query_sum + gradients[3]
        map_key_sum = map_key_sum + gradients[4]
    map_key = lax.optimization_barrier(jnp.sum(map_key_sum.reshape(kv_count, GROUP, key_map.shape[1], key_map.shape[2]), axis=1))
    return (jnp.stack(query_grads), jnp.stack(key_grads), jnp.stack(value_grads), map_query_sum, map_key)
```

```python
import math

import jax
import jax.numpy as jnp
from jax import lax
from jax.experimental import pallas as pl
from jax.experimental.pallas import tpu as pltpu
from jax.sharding import Mesh
from jax.sharding import PartitionSpec as P

CTX = ("ctx_0", "ctx_1")
DP_CTX = ("dp", "ctx_0", "ctx_1")
F32 = jnp.float32
BF16 = jnp.bfloat16
LOG2E = 1.0 / math.log(2.0)
TOK = 256
WID = 128
GRP = 8
KVH = 2
HEADS = GRP * KVH
STEP = 2
N_CTX = 16
SROWS = WID + 8


def split(x):
    hi = x.astype(BF16)
    return hi, (x - hi.astype(F32)).astype(BF16)


def dot(a, b, ca, cb):
    return lax.dot_general(a, b, (((ca,), (cb,)), ((), ())), preferred_element_type=F32)


def deep(a, b, ca, cb):
    ah, al = a
    bh, bl = b
    return dot(jnp.concatenate([ah, al], ca), jnp.concatenate([bh, bh], cb), ca, cb) + dot(ah, bl, ca, cb)


def wide(a, b, ca, cb):
    ah, al = a
    bh, bl = b
    n = bh.shape[1 - cb]
    both = dot(ah, jnp.concatenate([bh, bl], 1 - cb), ca, cb)
    return both[:, :n] + both[:, n:] + dot(al, bh, ca, cb)


def softmax(x):
    e = jnp.exp(x - jnp.max(x, axis=-1, keepdims=True))
    return e / jnp.sum(e, axis=-1, keepdims=True)


def local_kernel(q_ref, k_ref, v_ref, w_ref, wk_ref, qf_ref, num_ref, acc_ref, stat_ref, a_ref, kf_ref):
    @pl.when(pl.program_id(0) % (GRP // STEP) == 0)
    def _():
        kf_ref[0] = softmax(deep(split(k_ref[0]), split(wk_ref[0]), 1, 0))

    k, v, kf = split(k_ref[0]), split(v_ref[0]), split(kf_ref[0])
    causal = lax.broadcasted_iota(jnp.int32, (TOK, TOK), 0) >= lax.broadcasted_iota(jnp.int32, (TOK, TOK), 1)
    lane = lax.broadcasted_iota(jnp.int32, (TOK, WID), 1)
    for i in range(STEP):
        q = q_ref[i]
        qf = softmax(deep(split(q), split(w_ref[i]), 1, 0))
        qf_ref[i] = qf
        a = jnp.where(causal, deep(split(qf), kf, 1, 1), 0.0)
        a_ref[i] = a
        num_ref[i] = wide(split(a), v, 1, 0)
        den = jnp.sum(a, axis=-1, keepdims=True)
        s = deep(split(q * (LOG2E / math.sqrt(WID))), k, 1, 1)
        s = jnp.where(causal, s, -1e30)
        m = jnp.max(s, axis=-1, keepdims=True)
        p = jnp.where(causal, jnp.exp2(s - m), 0.0)
        acc_ref[i] = wide(split(p), v, 1, 0)
        l = jnp.sum(p, axis=-1, keepdims=True)
        stat_ref[i] = jnp.where(lane == 0, m, jnp.where(lane == 1, l, den))


def teacher_kernel(pos, q_ref, acc0_ref, stat_ref, kv_ref, wk_ref, t_ref, sq_ref, p_ref, n_ref, buf, sem, qs, m_sc, l_sc, acc):
    first, own = pos[0], pos[1]
    rows = STEP * TOK
    tiles = GRP // STEP

    def fetch(j, slot):
        return pltpu.make_async_copy(kv_ref.at[j], buf.at[slot], sem.at[slot])

    @pl.when(first < own)
    def _():
        fetch(first, 0).start()

    lane = lax.broadcasted_iota(jnp.int32, (rows, WID), 1)
    for i in range(tiles):
        here = pl.ds(i * rows, rows)
        q = q_ref[i * STEP : (i + 1) * STEP].reshape(rows, WID) * (LOG2E / math.sqrt(WID))
        hi, lo = split(q)
        qs[here, :WID] = hi
        qs[here, WID:] = lo
        stat = stat_ref[i * STEP : (i + 1) * STEP].reshape(rows, WID)
        m_sc[here, :] = jnp.broadcast_to(stat[:, 0:1], (rows, WID))
        l_sc[here, :] = jnp.where(lane == 1, stat, 0.0)
        acc[here, :] = acc0_ref[i * STEP : (i + 1) * STEP].reshape(rows, WID)
    p_ref[...] = jnp.zeros_like(p_ref)
    n_ref[...] = jnp.zeros_like(n_ref)
    wk = split(wk_ref[0])

    def visit(j, carry):
        slot = lax.rem(j - first, 2)
        fetch(j, slot).wait()

        @pl.when(j + 1 < own)
        def _():
            fetch(j + 1, 1 - slot).start()

        kh, kl = split(buf[slot, 0])
        vh, vl = split(buf[slot, 1])
        k_twice = jnp.concatenate([kh, kh], 1)
        v_both = jnp.concatenate([vh, vl], 1)
        kf = softmax(deep((kh, kl), wk, 1, 0))
        p_ref[...] += wide(split(kf), (vh, vl), 0, 0)
        n_ref[...] += jnp.broadcast_to(jnp.sum(kf, axis=0, keepdims=True), n_ref.shape)
        for i in range(tiles):
            here = pl.ds(i * rows, rows)
            q = qs[here, :]
            s = dot(q, k_twice, 1, 1) + dot(q[:, :WID], kl, 1, 1)
            m_old = m_sc[here, :]
            m_new = jnp.maximum(m_old, jnp.max(s, axis=-1, keepdims=True))
            p = jnp.exp2(s - jnp.concatenate([m_new, m_new], 1))
            fade = jnp.exp2(m_old - m_new)
            m_sc[here, :] = m_new
            l_sc[here, :] = fade * l_sc[here, :] + p[:, :WID] + p[:, WID:]
            ph, pl_ = split(p)
            both = dot(ph, v_both, 1, 0)
            acc[here, :] = fade * acc[here, :] + both[:, :WID] + both[:, WID:] + dot(pl_, vh, 1, 0)
        return carry

    lax.fori_loop(first, own, visit, 0)
    total = jnp.zeros((TOK, WID), F32)
    for i in range(tiles):
        here = pl.ds(i * rows, rows)
        t = acc[here, :] / jnp.sum(l_sc[here, :], axis=-1, keepdims=True)
        t_ref[i * STEP : (i + 1) * STEP] = t.reshape(STEP, TOK, WID)
        for k in range(STEP):
            part = t[k * TOK : (k + 1) * TOK]
            total = total + part * part
    line = jnp.sum(total, axis=-1, keepdims=True)
    sq_ref[...] = jnp.transpose(jnp.broadcast_to(line, (TOK, WID)))[:8]


def student_kernel(
    pos, q_ref, qf_ref, num_ref, stat_ref, a_ref, t0_ref, t1_ref, w_ref, k_ref, v_ref, kf_ref, p0_ref, p1_ref,
    n0_ref, n1_ref, sq0_ref, sq1_ref, sq2_ref, sq3_ref, wk_ref, kv0_ref, kv1_ref,
    gq_ref, mq_ref, gkf_ref, gv_ref, s_ref, mk_ref, buf, sem,
):
    step = pl.program_id(0)
    per = GRP // STEP
    head = step // per
    first, own = pos[0], pos[1]

    @pl.when(step % per == 0)
    def _():
        gkf_ref[...] = jnp.zeros_like(gkf_ref)
        gv_ref[...] = jnp.zeros_like(gv_ref)
        s_ref[...] = jnp.zeros_like(s_ref)

    low = head == 0
    prior = split(jnp.where(low, p0_ref[...], p1_ref[...]))
    prior_n = jnp.where(low, n0_ref[...], n1_ref[...])[:1]
    v, kf = split(v_ref[0]), split(kf_ref[0])
    squares = sq0_ref[...] + sq1_ref[...] + sq2_ref[...] + sq3_ref[...]
    mean = squares / (4 * HEADS * WID) + 1e-6
    scale = jnp.transpose(2.0 / mean)[:, 0:1]
    causal = lax.broadcasted_iota(jnp.int32, (TOK, TOK), 0) >= lax.broadcasted_iota(jnp.int32, (TOK, TOK), 1)
    for i in range(STEP):
        qf = qf_ref[i]
        qfs = split(qf)
        teacher = jnp.where(low, t0_ref[i], t1_ref[i])
        num = num_ref[i] + deep(qfs, prior, 1, 0)
        den = stat_ref[i][:, 2:3] + jnp.sum(qf * prior_n, axis=-1, keepdims=True)
        inv = 1.0 / den
        student = num * inv
        gn = (student - teacher) * (scale * inv)
        gd = -jnp.sum(gn * student, axis=-1, keepdims=True)
        gns = split(gn)
        gs = jnp.where(causal, deep(gns, v, 1, 1) + gd, 0.0)
        gss = split(gs)
        gqf = deep(gns, prior, 1, 1) + gd * prior_n + wide(gss, kf, 1, 0)
        qlg = qf * (gqf - jnp.sum(qf * gqf, axis=-1, keepdims=True))
        qlgs = split(qlg)
        gq_ref[i] = deep(qlgs, split(w_ref[i]), 1, 1)
        mq_ref[i] = wide(split(q_ref[i]), qlgs, 0, 0)
        gkf_ref[0] += wide(gss, qfs, 0, 0)
        gv_ref[0] += wide(split(a_ref[i]), gns, 0, 0)
        s_ref[0, :WID] += wide(qfs, gns, 0, 0)
        s_ref[0, WID:] += jnp.broadcast_to(jnp.sum(qf * gd, axis=0, keepdims=True), (8, WID))

    def key_map_part(kv_ref):
        state = split(s_ref[0, :WID])
        norm = s_ref[0, WID : WID + 1]
        wk = split(wk_ref[0])

        def fetch(j, slot):
            return pltpu.make_async_copy(kv_ref.at[j], buf.at[slot], sem.at[slot])

        @pl.when(first < own)
        def _():
            fetch(first, 0).start()

        def logit_grad(feats, grad):
            return feats * (grad - jnp.sum(feats * grad, axis=-1, keepdims=True))

        mk_ref[0] = wide(split(k_ref[0]), split(logit_grad(kf_ref[0], gkf_ref[0])), 0, 0)

        def visit(j, carry):
            slot = lax.rem(j - first, 2)
            fetch(j, slot).wait()

            @pl.when(j + 1 < own)
            def _():
                fetch(j + 1, 1 - slot).start()

            ks = split(buf[slot, 0])
            feats = softmax(deep(ks, wk, 1, 0))
            grad = deep(split(buf[slot, 1]), state, 1, 1) + norm
            mk_ref[0] += wide(ks, split(logit_grad(feats, grad)), 0, 0)
            return carry

        lax.fori_loop(first, own, visit, 0)

    @pl.when(step == per - 1)
    def _():
        key_map_part(kv0_ref)

    @pl.when(step == 2 * per - 1)
    def _():
        key_map_part(kv1_ref)


def later_kernel(pos, s_ref, gkf_ref, gv_ref, kf_ref, v_ref, wk_ref, gk_ref, out_ref):
    own, last = pos[1], pos[2]
    for h in range(KVH):
        total = lax.fori_loop(
            own + 1, last + 1, lambda j, held: held + s_ref[j, h], jnp.zeros((SROWS, WID), F32)
        )
        state, norm = split(total[:WID]), total[WID : WID + 1]
        kf = kf_ref[h]
        gkf = gkf_ref[h] + deep(split(v_ref[h]), state, 1, 1) + norm
        out_ref[h] = gv_ref[h] + deep(split(kf), state, 1, 0)
        klg = kf * (gkf - jnp.sum(kf * gkf, axis=-1, keepdims=True))
        gk_ref[h] = deep(split(klg), split(wk_ref[h]), 1, 1)


def shape(*dims):
    return jax.ShapeDtypeStruct(dims, F32)


def full(*dims):
    return pl.BlockSpec(dims, lambda *_: (0,) * len(dims))


def params(limit=56):
    return pltpu.CompilerParams(vmem_limit_bytes=limit * 1024 * 1024)


def body(queries, key_rows, value_rows, query_map, key_map, block_doc):
    keys = jnp.transpose(key_rows[0], (1, 0, 2))
    values = jnp.transpose(value_rows[0], (1, 0, 2))
    gathered = []
    for h in range(KVH):
        pair = jnp.stack([keys[h], values[h]])
        gathered.append(lax.all_gather(pair, CTX))

    own = lax.axis_index(CTX).astype(jnp.int32)
    doc_table = block_doc[0]
    places = jnp.arange(N_CTX, dtype=jnp.int32)
    own_doc = jnp.sum(jnp.where(places == own, doc_table, 0))
    first = jnp.sum((doc_table < own_doc).astype(jnp.int32))
    last = jnp.sum((doc_table <= own_doc).astype(jnp.int32)) - 1
    pos = jnp.stack([first, own, last])

    q = jnp.transpose(queries[0], (1, 0, 2))
    per = GRP // STEP
    by_head = lambda *dims: pl.BlockSpec((STEP, *dims), lambda g, *_: (g, 0, 0))
    by_kv = lambda *dims: pl.BlockSpec((1, *dims), lambda g, *_: (g // per, 0, 0))
    qf, num, acc0, stat, a, kf = pl.pallas_call(
        local_kernel,
        grid=(HEADS // STEP,),
        in_specs=[by_head(TOK, WID), by_kv(TOK, WID), by_kv(TOK, WID), by_head(WID, WID), by_kv(WID, WID)],
        out_specs=[by_head(TOK, WID)] * 4 + [by_head(TOK, TOK), by_kv(TOK, WID)],
        out_shape=[shape(HEADS, TOK, WID)] * 4 + [shape(HEADS, TOK, TOK), shape(KVH, TOK, WID)],
        compiler_params=params(),
        name="local",
    )(q, keys, values, query_map, key_map)

    any_spec = pl.BlockSpec(memory_space=pl.ANY)
    parts = []
    for h in range(KVH):
        of = lambda *dims, h=h: pl.BlockSpec((GRP, *dims), lambda g, *_: (h, 0, 0))
        parts.append(
            pl.pallas_call(
                teacher_kernel,
                grid_spec=pltpu.PrefetchScalarGridSpec(
                    num_scalar_prefetch=1,
                    grid=(1,),
                    in_specs=[
                        of(TOK, WID),
                        of(TOK, WID),
                        of(TOK, WID),
                        any_spec,
                        pl.BlockSpec((1, WID, WID), lambda g, *_, h=h: (h, 0, 0)),
                    ],
                    out_specs=[full(GRP, TOK, WID), full(8, TOK), full(WID, WID), full(8, WID)],
                    scratch_shapes=[
                        pltpu.VMEM((2, 2, TOK, WID), F32),
                        pltpu.SemaphoreType.DMA((2,)),
                        pltpu.VMEM((GRP * TOK, 2 * WID), BF16),
                        pltpu.VMEM((GRP * TOK, WID), F32),
                        pltpu.VMEM((GRP * TOK, WID), F32),
                        pltpu.VMEM((GRP * TOK, WID), F32),
                    ],
                ),
                out_shape=[shape(GRP, TOK, WID), shape(8, TOK), shape(WID, WID), shape(8, WID)],
                compiler_params=params(),
                name="teacher",
            )(pos, q, acc0, stat, gathered[h], key_map)
        )
    (t0, sq_a, p0, n0), (t1, sq_b, p1, n1) = parts
    squares = sq_a + sq_b
    others = [lax.ppermute(squares, "head", [(i, (i + k) % 4) for i in range(4)]) for k in (1, 2, 3)]

    half = lambda c: pl.BlockSpec(
        (STEP, TOK, WID), lambda g, *_: ((jnp.minimum(g, per - 1) if c == 0 else jnp.maximum(g - per, 0)), 0, 0)
    )
    gq, mq, gkf, gv, states, mk = pl.pallas_call(
        student_kernel,
        grid_spec=pltpu.PrefetchScalarGridSpec(
            num_scalar_prefetch=1,
            grid=(HEADS // STEP,),
            in_specs=[
                by_head(TOK, WID), by_head(TOK, WID), by_head(TOK, WID), by_head(TOK, WID), by_head(TOK, TOK),
                half(0), half(1), by_head(WID, WID), by_kv(TOK, WID), by_kv(TOK, WID), by_kv(TOK, WID),
                full(WID, WID), full(WID, WID), full(8, WID), full(8, WID),
                full(8, TOK), full(8, TOK), full(8, TOK), full(8, TOK),
                by_kv(WID, WID), any_spec, any_spec,
            ],
            out_specs=[
                by_head(TOK, WID), by_head(WID, WID), by_kv(TOK, WID), by_kv(TOK, WID), by_kv(SROWS, WID),
                by_kv(WID, WID),
            ],
            scratch_shapes=[pltpu.VMEM((2, 2, TOK, WID), F32), pltpu.SemaphoreType.DMA((2,))],
        ),
        out_shape=[
            shape(HEADS, TOK, WID), shape(HEADS, WID, WID), shape(KVH, TOK, WID), shape(KVH, TOK, WID),
            shape(KVH, SROWS, WID), shape(KVH, WID, WID),
        ],
        compiler_params=params(),
        name="student",
    )(pos, q, qf, num, stat, a, t0, t1, query_map, keys, values, kf, p0, p1, n0, n1,
      squares, *others, key_map, *gathered)

    all_states = lax.all_gather(states, CTX)
    maps = jnp.concatenate([mq, mk]).reshape(32, -1, WID)
    maps = jnp.sum(lax.all_to_all(maps, DP_CTX, 0, 0, tiled=True), axis=0)
    maps = lax.all_to_all(jnp.broadcast_to(maps, (32, *maps.shape)), DP_CTX, 0, 0, tiled=True)
    maps = maps.reshape(HEADS + KVH, WID, WID)

    grad_keys, grad_values = pl.pallas_call(
        later_kernel,
        grid_spec=pltpu.PrefetchScalarGridSpec(
            num_scalar_prefetch=1,
            grid=(1,),
            in_specs=[full(N_CTX, KVH, SROWS, WID)] + [full(KVH, TOK, WID)] * 4 + [full(KVH, WID, WID)],
            out_specs=[full(KVH, TOK, WID)] * 2,
        ),
        out_shape=[shape(KVH, TOK, WID)] * 2,
        compiler_params=params(),
        name="later",
    )(pos, all_states, gkf, gv, kf, values, key_map)
    back = lambda x: jnp.transpose(x, (1, 0, 2))[None]
    return (back(gq), back(grad_keys), back(grad_values), maps[:HEADS], maps[HEADS:])


def solution(mesh):
    torus = Mesh(
        mesh.devices.reshape(mesh.shape["dp"], 4, 4, mesh.shape["head"]),
        ("dp", "ctx_0", "ctx_1", "head"),
    )
    rows = P("dp", CTX, "head", None)
    placed = (rows, rows, rows, P("head", None, None), P("head", None, None), P("dp", None))
    return jax.shard_map(
        body, mesh=torus, in_specs=placed, out_specs=(rows, rows, rows, placed[3], placed[4]), check_vma=False
    )
```

```python
import functools
import math

import jax
import jax.numpy as jnp
from jax import lax
from jax.experimental import pallas as pl
from jax.experimental.pallas import tpu as pltpu
from jax.sharding import Mesh
from jax.sharding import PartitionSpec as P


CTX = ("ctx_0", "ctx_1")
DP_CTX = ("dp", "ctx_0", "ctx_1")
F32 = jnp.float32
BF16 = jnp.bfloat16
LOG2E = 1.0 / math.log(2.0)
TOK = 256
WID = 128
GRP = 8
KVH = 2
HEADS = GRP * KVH
STEP = 2
WIDE = 8
TILE = 2
N_CTX = 16
SROWS = WID + 8


def split(x):
    hi = x.astype(BF16)
    return hi, (x - hi.astype(F32)).astype(BF16)


def dot(a, b, ca, cb):
    return lax.dot_general(a, b, (((ca,), (cb,)), ((), ())), preferred_element_type=F32)


def deep(a, b, ca, cb):
    ah, al = a
    bh, bl = b
    return dot(jnp.concatenate([ah, al], ca), jnp.concatenate([bh, bh], cb), ca, cb) + dot(ah, bl, ca, cb)


def wide(a, b, ca, cb):
    ah, al = a
    bh, bl = b
    n = bh.shape[1 - cb]
    both = dot(ah, jnp.concatenate([bh, bl], 1 - cb), ca, cb)
    return both[:, :n] + both[:, n:] + dot(al, bh, ca, cb)


def softmax(x):
    e = jnp.exp(x - jnp.max(x, axis=-1, keepdims=True))
    return e / jnp.sum(e, axis=-1, keepdims=True)


SOURCES = ((0, 3), (0, 1), (1, 0), (1, 3), (1, 1), (2, 0), (0, 2), (2, 3), (2, 1), (1, 2), (2, 2))


def bounds(docs):
    own = 4 * lax.axis_index("ctx_0") + lax.axis_index("ctx_1")
    first, last = 0, -1
    for j in range(N_CTX):
        first = first + (docs[j] < docs[own]).astype(jnp.int32)
        last = last + (docs[j] <= docs[own]).astype(jnp.int32)
    return first, own, last


def note_wanted(docs, flags, places):
    row, column = lax.axis_index("ctx_0"), lax.axis_index("ctx_1")
    own = 4 * row + column
    for k, place in enumerate(places):
        back, on = SOURCES[place]
        source = 4 * (row - back) + lax.rem(column + on, 4)
        seen = (source >= 0) & (source < own)
        flags[k] = (seen & (docs[jnp.maximum(source, 0)] == docs[own])).astype(jnp.int32)


def local_kernel(q_ref, k_ref, v_ref, w_ref, wk_ref, *refs):
    qf_ref, num_ref, acc_ref, stat_ref, a_ref, kf_ref, s_ref = refs[-7:]

    @pl.when(pl.program_id(0) == 0)
    def _():
        kf = softmax(deep(split(k_ref[0]), split(wk_ref[0]), 1, 0))
        kf_ref[0] = kf
        s_ref[0, :WID] = wide(split(kf), split(v_ref[0]), 0, 0)
        s_ref[0, WID:] = jnp.broadcast_to(jnp.sum(kf, axis=0, keepdims=True), (8, WID))

    k, v, kf = split(k_ref[0]), split(v_ref[0]), split(kf_ref[0])
    causal = lax.broadcasted_iota(jnp.int32, (TOK, TOK), 0) >= lax.broadcasted_iota(jnp.int32, (TOK, TOK), 1)
    lane = lax.broadcasted_iota(jnp.int32, (TOK, WID), 1)
    for i in range(STEP):
        q = q_ref[i]
        qf = softmax(deep(split(q), split(w_ref[i]), 1, 0))
        qf_ref[i] = qf
        a = jnp.where(causal, deep(split(qf), kf, 1, 1), 0.0)
        a_ref[i] = a
        num_ref[i] = wide(split(a), v, 1, 0)
        den = jnp.sum(a, axis=-1, keepdims=True)
        s = deep(split(q * (LOG2E / math.sqrt(WID))), k, 1, 1)
        s = jnp.where(causal, s, -1e30)
        m = jnp.max(s, axis=-1, keepdims=True)
        p = jnp.where(causal, jnp.exp2(s - m), 0.0)
        acc_ref[i] = wide(split(p), v, 1, 0)
        l = jnp.sum(p, axis=-1, keepdims=True)
        stat_ref[i] = jnp.where(lane == 0, m, jnp.where(lane == 1, l, den))


def attend_kernel(whole, halves, final, at, docs, q_ref, acc0_ref, stat_ref, *refs):
    count = whole + halves
    pieces, refs = refs[: whole + 2 * halves], refs[whole + 2 * halves :]
    if final:
        t_ref, sq_ref, flags, buf, sem, keys, values, qs, m_sc, l_sc, acc = refs
    else:
        acc_out, stat_out, flags, buf, sem, keys, values, qs, m_sc, l_sc, acc = refs
    g = pl.program_id(0)
    head = g // (GRP // WIDE)

    def copies(k):
        if k < whole:
            return [pltpu.make_async_copy(pieces[k], buf.at[k], sem.at[k, 0])]
        pair = pieces[whole + 2 * (k - whole) : whole + 2 * (k - whole) + 2]
        return [pltpu.make_async_copy(pair[h], buf.at[k, h], sem.at[k, h]) for h in range(KVH)]

    @pl.when(g == 0)
    def _():
        note_wanted(docs, flags, range(at, at + count))
        for k in range(count):

            @pl.when(flags[k] == 1)
            def _(k=k):
                for copy in copies(k):
                    copy.start()

    rows = TILE * TOK
    tiles = WIDE // TILE
    lane = lax.broadcasted_iota(jnp.int32, (rows, WID), 1)
    for i in range(tiles):
        here = pl.ds(i * rows, rows)
        q = q_ref[i * TILE : (i + 1) * TILE].reshape(rows, WID) * (LOG2E / math.sqrt(WID))
        hi, lo = split(q)
        qs[here, :WID] = hi
        qs[here, WID:] = lo
        stat = stat_ref[i * TILE : (i + 1) * TILE].reshape(rows, WID)
        m_sc[here, :] = jnp.broadcast_to(stat[:, 0:1], (rows, WID))
        l_sc[here, :] = jnp.where(lane == 1, stat, 0.0)
        acc[here, :] = acc0_ref[i * TILE : (i + 1) * TILE].reshape(rows, WID)

    @pl.when(g == 0)
    def _():
        for k in range(count):

            @pl.when(flags[k] == 1)
            def _(k=k):
                for copy in copies(k):
                    copy.wait()

        def divide(n, carry):
            k, h = n // KVH, n % KVH
            keys[k, h, :, :WID], keys[k, h, :, WID:] = split(buf[k, h, 0])
            values[k, h, :, :WID], values[k, h, :, WID:] = split(buf[k, h, 1])
            return carry

        lax.fori_loop(0, count * KVH, divide, 0)

    def visit(k, carry):
        @pl.when(flags[k] == 1)
        def _():
            kh, kl = keys[k, head, :, :WID], keys[k, head, :, WID:]
            v_both = values[k, head]
            k_twice = jnp.concatenate([kh, kh], 1)
            for i in range(tiles):
                here = pl.ds(i * rows, rows)
                q = qs[here, :]
                s = dot(q, k_twice, 1, 1) + dot(q[:, :WID], kl, 1, 1)
                m_old = m_sc[here, :]
                m_new = jnp.maximum(m_old, jnp.max(s, axis=-1, keepdims=True))
                p = jnp.exp2(s - jnp.concatenate([m_new, m_new], 1))
                fade = jnp.exp2(m_old - m_new)
                m_sc[here, :] = m_new
                l_sc[here, :] = fade * l_sc[here, :] + p[:, :WID] + p[:, WID:]
                ph, pl_ = split(p)
                both = dot(ph, v_both, 1, 0)
                acc[here, :] = (
                    fade * acc[here, :] + both[:, :WID] + both[:, WID:] + dot(pl_, v_both[:, :WID], 1, 0)
                )

        return carry

    lax.fori_loop(0, count, visit, 0)
    if not final:
        for i in range(tiles):
            here = pl.ds(i * rows, rows)
            acc_out[i * TILE : (i + 1) * TILE] = acc[here, :].reshape(TILE, TOK, WID)
            stat = stat_ref[i * TILE : (i + 1) * TILE].reshape(rows, WID)
            l = jnp.sum(l_sc[here, :], axis=-1, keepdims=True)
            stat = jnp.where(lane == 0, m_sc[here, :], jnp.where(lane == 1, l, stat))
            stat_out[i * TILE : (i + 1) * TILE] = stat.reshape(TILE, TOK, WID)
        return
    total = jnp.zeros((TOK, WID), F32)
    for i in range(tiles):
        here = pl.ds(i * rows, rows)
        t = acc[here, :] / jnp.sum(l_sc[here, :], axis=-1, keepdims=True)
        t_ref[i * TILE : (i + 1) * TILE] = t.reshape(TILE, TOK, WID)
        for k in range(TILE):
            part = t[k * TOK : (k + 1) * TOK]
            total = total + part * part
    line = jnp.sum(total, axis=-1, keepdims=True)
    line = jnp.transpose(jnp.broadcast_to(line, (TOK, WID)))[:8]

    @pl.when(g == 0)
    def _():
        sq_ref[...] = line

    @pl.when(g > 0)
    def _():
        sq_ref[...] += line


def student_kernel(
    docs, q_ref, qf_ref, num_ref, stat_ref, a_ref, t_ref, w_ref, v_ref, kf_ref, states_ref,
    sq0_ref, sq1_ref, sq2_ref, sq3_ref, gq_ref, mq_ref, gkf_ref, gv_ref, s_ref, prior_ref,
):
    step = pl.program_id(0)
    per = GRP // STEP

    @pl.when(step % per == 0)
    def _():
        gkf_ref[...] = jnp.zeros_like(gkf_ref)
        gv_ref[...] = jnp.zeros_like(gv_ref)
        s_ref[...] = jnp.zeros_like(s_ref)
        first, own, _ = bounds(docs)
        prior_ref[...] = lax.fori_loop(
            first, own, lambda j, held: held + states_ref[j, 0], jnp.zeros((SROWS, WID), F32)
        )

    prior = split(prior_ref[:WID])
    prior_n = prior_ref[WID : WID + 1]
    v, kf = split(v_ref[0]), split(kf_ref[0])
    squares = sq0_ref[...] + sq1_ref[...] + sq2_ref[...] + sq3_ref[...]
    mean = squares / (4 * HEADS * WID) + 1e-6
    scale = jnp.transpose(2.0 / mean)[:, 0:1]
    causal = lax.broadcasted_iota(jnp.int32, (TOK, TOK), 0) >= lax.broadcasted_iota(jnp.int32, (TOK, TOK), 1)
    for i in range(STEP):
        qf = qf_ref[i]
        qfs = split(qf)
        teacher = t_ref[i]
        num = num_ref[i] + deep(qfs, prior, 1, 0)
        den = stat_ref[i][:, 2:3] + jnp.sum(qf * prior_n, axis=-1, keepdims=True)
        inv = 1.0 / den
        student = num * inv
        gn = (student - teacher) * (scale * inv)
        gd = -jnp.sum(gn * student, axis=-1, keepdims=True)
        gns = split(gn)
        gs = jnp.where(causal, deep(gns, v, 1, 1) + gd, 0.0)
        gss = split(gs)
        gqf = deep(gns, prior, 1, 1) + gd * prior_n + wide(gss, kf, 1, 0)
        qlg = qf * (gqf - jnp.sum(qf * gqf, axis=-1, keepdims=True))
        qlgs = split(qlg)
        gq_ref[i] = deep(qlgs, split(w_ref[i]), 1, 1)
        mq_ref[i] = wide(split(q_ref[i]), qlgs, 0, 0)
        gkf_ref[0] += wide(gss, qfs, 0, 0)
        gv_ref[0] += wide(split(a_ref[i]), gns, 0, 0)
        s_ref[0, :WID] += wide(qfs, gns, 0, 0)
        s_ref[0, WID:] += jnp.broadcast_to(jnp.sum(qf * gd, axis=0, keepdims=True), (8, WID))


def key_map_kernel(docs, k_ref, kf_ref, gkf_ref, s_ref, wk_ref, *refs):
    pieces, (mk_ref, flags, buf, sem) = refs[:-4], refs[-4:]
    note_wanted(docs, flags, (0, 1, 2, 3, 4, 5, 7, 8, 6, 9, 10))
    state = [split(s_ref[h, :WID]) for h in range(KVH)]
    norm = [s_ref[h, WID : WID + 1] for h in range(KVH)]
    wk = [split(wk_ref[h]) for h in range(KVH)]

    def copies(k):
        if k < 8:
            return [pltpu.make_async_copy(pieces[k], buf.at[k], sem.at[k, 0])]
        return [pltpu.make_async_copy(pieces[2 * k - 8 + h], buf.at[k, h], sem.at[k, h]) for h in range(KVH)]

    for k in range(11):

        @pl.when(flags[k] == 1)
        def _(k=k):
            for copy in copies(k):
                copy.start()

    def logit_grad(feats, grad):
        return feats * (grad - jnp.sum(feats * grad, axis=-1, keepdims=True))

    for h in range(KVH):
        mk_ref[h] = wide(split(k_ref[h]), split(logit_grad(kf_ref[h], gkf_ref[h])), 0, 0)
    for k in range(11):

        @pl.when(flags[k] == 1)
        def _(k=k):
            for copy in copies(k):
                copy.wait()

    def visit(k, carry):
        @pl.when(flags[k] == 1)
        def _():
            for h in range(KVH):
                ks = split(buf[k, h, 0])
                feats = softmax(deep(ks, wk[h], 1, 0))
                grad = deep(split(buf[k, h, 1]), state[h], 1, 1) + norm[h]
                mk_ref[h] += wide(ks, split(logit_grad(feats, grad)), 0, 0)

        return carry

    lax.fori_loop(0, 11, visit, 0)


def later_kernel(docs, s_ref, gkf_ref, gv_ref, kf_ref, v_ref, wk_ref, gk_ref, out_ref):
    _, own, last = bounds(docs)
    for h in range(KVH):
        total = lax.fori_loop(
            own + 1, last + 1, lambda j, held: held + s_ref[j, h], jnp.zeros((SROWS, WID), F32)
        )
        state, norm = split(total[:WID]), total[WID : WID + 1]
        kf = kf_ref[h]
        gkf = gkf_ref[h] + deep(split(v_ref[h]), state, 1, 1) + norm
        out_ref[h] = gv_ref[h] + deep(split(kf), state, 1, 0)
        klg = kf * (gkf - jnp.sum(kf * gkf, axis=-1, keepdims=True))
        gk_ref[h] = deep(split(klg), split(wk_ref[h]), 1, 1)


def shape(*dims):
    return jax.ShapeDtypeStruct(dims, F32)


def full(*dims):
    return pl.BlockSpec(dims, lambda *_: (0,) * len(dims))


def params(limit=56):
    return pltpu.CompilerParams(vmem_limit_bytes=limit * 1024 * 1024)


def cost(us):
    return pl.CostEstimate(flops=int(us * 1e9), bytes_accessed=int(us * 3e5), transcendentals=0)


def body(queries, key_rows, value_rows, query_map, key_map, block_doc):
    keys = jnp.transpose(key_rows[0], (1, 0, 2))
    values = jnp.transpose(value_rows[0], (1, 0, 2))
    mine = jnp.stack([keys, values], 1)
    down = lambda x: lax.ppermute(x, "ctx_0", [(i, i + 1) for i in range(3)])
    right = lambda x: lax.ppermute(x, "ctx_1", [(i, (i + 1) % 4) for i in range(4)])
    left = lambda x: lax.ppermute(x, "ctx_1", [(i, (i - 1) % 4) for i in range(4)])
    docs = block_doc[0]
    q = jnp.transpose(queries[0], (1, 0, 2))
    per = GRP // STEP
    by_head = lambda *dims: pl.BlockSpec((STEP, *dims), lambda g, *_: (g, 0, 0))
    by_kv = lambda *dims: pl.BlockSpec((1, *dims), lambda g, *_: (g // per, 0, 0))

    any_spec = pl.BlockSpec(memory_space=pl.ANY)

    def local(h, held):
        part = lambda *dims: pl.BlockSpec((STEP, *dims), lambda g: (g + h * per, 0, 0))
        kv = lambda *dims: pl.BlockSpec((1, *dims), lambda g: (h, 0, 0))
        return pl.pallas_call(
            local_kernel,
            grid=(per,),
            in_specs=[part(TOK, WID), kv(TOK, WID), kv(TOK, WID), part(WID, WID), kv(WID, WID)]
            + [any_spec] * len(held),
            out_specs=[part(TOK, WID)] * 4 + [part(TOK, TOK), kv(TOK, WID), kv(SROWS, WID)],
            out_shape=[shape(HEADS, TOK, WID)] * 4
            + [shape(HEADS, TOK, TOK), shape(KVH, TOK, WID), shape(KVH, SROWS, WID)],
            input_output_aliases={5 + i: i for i in range(len(held))},
            compiler_params=params(),
            cost_estimate=cost(8),
            name="local",
        )(q, keys, values, query_map, key_map, *held)

    arrived = down(mine), right(mine), left(mine)
    held = local(0, ())
    (za, yp0, ym0), held = lax.optimization_barrier((arrived, held))
    zb, yp1, ym1 = down(za), right(za), left(za)
    yp2, ym2 = right(zb), left(zb)
    across = [(right(p[0]), left(m[1])) for p, m in ((yp0, ym0), (yp1, ym1), (yp2, ym2))]

    qf, num, acc, stat, a, kf, states = local(1, held)
    block_states = lax.all_gather(states, CTX)

    wide_head = lambda *dims: pl.BlockSpec((WIDE, *dims), lambda g, *_: (g, 0, 0))

    def attend(acc, stat, whole, halves, at, final, us):
        count = len(whole) + len(halves)
        return pl.pallas_call(
            functools.partial(attend_kernel, len(whole), len(halves), final, at),
            grid_spec=pltpu.PrefetchScalarGridSpec(
                num_scalar_prefetch=1,
                grid=(HEADS // WIDE,),
                in_specs=[wide_head(TOK, WID)] * 3 + [any_spec] * (len(whole) + 2 * len(halves)),
                out_specs=[wide_head(TOK, WID), full(8, TOK) if final else wide_head(TOK, WID)],
                scratch_shapes=[
                    pltpu.SMEM((count,), jnp.int32),
                    pltpu.VMEM((count, KVH, 2, TOK, WID), F32),
                    pltpu.SemaphoreType.DMA((count, KVH)),
                    pltpu.VMEM((count, KVH, TOK, 2 * WID), BF16),
                    pltpu.VMEM((count, KVH, TOK, 2 * WID), BF16),
                    pltpu.VMEM((WIDE * TOK, 2 * WID), BF16),
                ]
                + [pltpu.VMEM((WIDE * TOK, WID), F32)] * 3,
            ),
            out_shape=[shape(HEADS, TOK, WID), shape(8, TOK) if final else shape(HEADS, TOK, WID)],
            compiler_params=params(26),
            cost_estimate=cost(us),
            name="attend",
        )(docs, q, acc, stat, *whole, *[x for pair in halves for x in pair])

    acc, stat = attend(acc, stat, [yp0, ym0, za], [], 0, False, 14)
    acc, stat = attend(acc, stat, [yp1, ym1, zb], [across[0]], 3, False, 16)
    acc, stat = attend(acc, stat, [yp2, ym2], [across[1]], 7, False, 12)
    teacher, squares = attend(acc, stat, [], [across[2]], 10, True, 6)
    others = [lax.ppermute(squares, "head", [(i, (i + k) % 4) for i in range(4)]) for k in (1, 2, 3)]

    gq, mq, gkf, gv, states = pl.pallas_call(
        student_kernel,
        grid_spec=pltpu.PrefetchScalarGridSpec(
            num_scalar_prefetch=1,
            grid=(HEADS // STEP,),
            in_specs=[
                by_head(TOK, WID), by_head(TOK, WID), by_head(TOK, WID), by_head(TOK, WID), by_head(TOK, TOK),
                by_head(TOK, WID), by_head(WID, WID), by_kv(TOK, WID), by_kv(TOK, WID),
                pl.BlockSpec((N_CTX, 1, SROWS, WID), lambda g, *_: (0, g // per, 0, 0)),
                full(8, TOK), full(8, TOK), full(8, TOK), full(8, TOK),
            ],
            out_specs=[by_head(TOK, WID), by_head(WID, WID), by_kv(TOK, WID), by_kv(TOK, WID), by_kv(SROWS, WID)],
            scratch_shapes=[pltpu.VMEM((SROWS, WID), F32)],
        ),
        out_shape=[
            shape(HEADS, TOK, WID), shape(HEADS, WID, WID), shape(KVH, TOK, WID), shape(KVH, TOK, WID),
            shape(KVH, SROWS, WID),
        ],
        compiler_params=params(),
        cost_estimate=cost(25),
        name="student",
    )(docs, q, qf, num, stat, a, teacher, query_map, values, kf, block_states, squares, *others)

    all_states = lax.all_gather(states, CTX)
    share = lambda x: jnp.sum(lax.all_to_all(x.reshape(32, -1, WID), DP_CTX, 0, 0, tiled=True), axis=0)
    query_part = share(mq)
    mk = pl.pallas_call(
        key_map_kernel,
        grid_spec=pltpu.PrefetchScalarGridSpec(
            num_scalar_prefetch=1,
            grid=(1,),
            in_specs=[full(KVH, TOK, WID)] * 3 + [full(KVH, SROWS, WID), full(KVH, WID, WID)] + [any_spec] * 14,
            out_specs=full(KVH, WID, WID),
            scratch_shapes=[pltpu.SMEM((11,), jnp.int32), pltpu.VMEM((11, KVH, 2, TOK, WID), F32), pltpu.SemaphoreType.DMA((11, KVH))],
        ),
        out_shape=shape(KVH, WID, WID),
        compiler_params=params(),
        cost_estimate=cost(10),
        name="key_map",
    )(docs, keys, kf, gkf, states, key_map,
      yp0, ym0, za, yp1, ym1, zb, yp2, ym2, *[x for pair in across for x in pair])
    mk, query_part = lax.optimization_barrier((mk, query_part))
    parts = jnp.concatenate([query_part, share(mk)])
    maps = lax.all_to_all(jnp.broadcast_to(parts, (32, *parts.shape)), DP_CTX, 0, 0, tiled=True)
    rows = HEADS * WID // 32
    grad_keys, grad_values = pl.pallas_call(
        later_kernel,
        grid_spec=pltpu.PrefetchScalarGridSpec(
            num_scalar_prefetch=1,
            grid=(1,),
            in_specs=[full(N_CTX, KVH, SROWS, WID)] + [full(KVH, TOK, WID)] * 4 + [full(KVH, WID, WID)],
            out_specs=[full(KVH, TOK, WID)] * 2,
        ),
        out_shape=[shape(KVH, TOK, WID)] * 2,
        compiler_params=params(),
        name="later",
    )(docs, all_states, gkf, gv, kf, values, key_map)
    back = lambda x: jnp.transpose(x, (1, 0, 2))[None]
    return (back(gq), back(grad_keys), back(grad_values), maps[:, :rows].reshape(mq.shape), maps[:, rows:].reshape(mk.shape))


def solution(mesh):
    torus = Mesh(
        mesh.devices.reshape(mesh.shape["dp"], 4, 4, mesh.shape["head"]),
        ("dp", "ctx_0", "ctx_1", "head"),
    )
    rows = P("dp", CTX, "head", None)
    placed = (rows, rows, rows, P("head", None, None), P("head", None, None), P("dp", None))
    return jax.shard_map(
        body, mesh=torus, in_specs=placed, out_specs=(rows, rows, rows, placed[3], placed[4]), check_vma=False
    )
```

```python
import functools
import math

import jax
import jax.numpy as jnp
from jax import lax
from jax.experimental import pallas as pl
from jax.experimental.pallas import tpu as pltpu
from jax.sharding import Mesh
from jax.sharding import PartitionSpec as P


CTX = ("ctx_0", "ctx_1")
DP_CTX = ("dp", "ctx_0", "ctx_1")
F32 = jnp.float32
BF16 = jnp.bfloat16
LOG2E = 1.0 / math.log(2.0)
TOK = 256
WID = 128
GRP = 8
KVH = 2
HEADS = GRP * KVH
STEP = 4
EARLY = 4
WIDE = 8
TILE = 2
N_CTX = 16
SROWS = WID + 8


def split(x):
    hi = x.astype(BF16)
    return hi, (x - hi.astype(F32)).astype(BF16)


def dot(a, b, ca, cb):
    return lax.dot_general(a, b, (((ca,), (cb,)), ((), ())), preferred_element_type=F32)


def deep(a, b, ca, cb):
    ah, al = a
    bh, bl = b
    return dot(jnp.concatenate([ah, al], ca), jnp.concatenate([bh, bh], cb), ca, cb) + dot(ah, bl, ca, cb)


def wide(a, b, ca, cb):
    ah, al = a
    bh, bl = b
    n = bh.shape[1 - cb]
    both = dot(ah, jnp.concatenate([bh, bl], 1 - cb), ca, cb)
    return both[:, :n] + both[:, n:] + dot(al, bh, ca, cb)


def softmax(x):
    e = jnp.exp(x - jnp.max(x, axis=-1, keepdims=True))
    return e / row_sum(e)


SOURCES = ((0, 3), (0, 1), (1, 0), (1, 3), (1, 1), (2, 0), (0, 2), (2, 3), (2, 1), (1, 2), (2, 2))


def bounds(docs):
    own = 4 * lax.axis_index("ctx_0") + lax.axis_index("ctx_1")
    first, last = 0, -1
    for j in range(N_CTX):
        first = first + (docs[j] < docs[own]).astype(jnp.int32)
        last = last + (docs[j] <= docs[own]).astype(jnp.int32)
    return first, own, last


def note_wanted(docs, flags, places):
    row, column = lax.axis_index("ctx_0"), lax.axis_index("ctx_1")
    own = 4 * row + column
    for k, place in enumerate(places):
        back, on = SOURCES[place]
        source = 4 * (row - back) + lax.rem(column + on, 4)
        seen = (source >= 0) & (source < own)
        flags[k] = (seen & (docs[jnp.maximum(source, 0)] == docs[own])).astype(jnp.int32)


HEAD_ROWS = [slice(i * TOK, (i + 1) * TOK) for i in range(GRP)]


def stacked_mask(heads):
    row = lax.broadcasted_iota(jnp.int32, (heads * TOK, TOK), 0)
    return lax.rem(row, TOK) >= lax.broadcasted_iota(jnp.int32, (heads * TOK, TOK), 1)


def row_sum(x):
    return dot(jnp.concatenate(split(x), 1), jnp.ones((2 * WID, WID), BF16), 1, 0)


def local_kernel(q_ref, k_ref, v_ref, w_ref, wk_ref, *refs):
    qf_ref, num_ref, acc_ref, stat_ref, a_ref, kf_ref, s_ref = refs[-7:]

    @pl.when(pl.program_id(0) == 0)
    def _():
        kf = softmax(deep(split(k_ref[0]), split(wk_ref[0]), 1, 0))
        kf_ref[0] = kf
        s_ref[0, :WID] = wide(split(kf), split(v_ref[0]), 0, 0)
        s_ref[0, WID:] = jnp.broadcast_to(jnp.sum(kf, axis=0, keepdims=True), (8, WID))

    k, v, kf = split(k_ref[0]), split(v_ref[0]), split(kf_ref[0])
    rows = EARLY * TOK
    causal = stacked_mask(EARLY)
    lane = lax.broadcasted_iota(jnp.int32, (rows, WID), 1)
    whole = lambda x: x.reshape(EARLY, TOK, x.shape[-1])
    q = q_ref[...].reshape(rows, WID)
    qh, ql = split(q)
    logits = [deep((qh[at], ql[at]), split(w_ref[i]), 1, 0) for i, at in enumerate(HEAD_ROWS[:EARLY])]
    qf = softmax(jnp.concatenate(logits, 0))
    qf_ref[...] = whole(qf)
    a = jnp.where(causal, deep(split(qf), kf, 1, 1), 0.0)
    a_ref[...] = whole(a)
    num_ref[...] = whole(wide(split(a), v, 1, 0))
    den = jnp.sum(a, axis=-1, keepdims=True)
    s = deep(split(q * (LOG2E / math.sqrt(WID))), k, 1, 1)
    s = jnp.where(causal, s, -1e30)
    m = jnp.max(s, axis=-1, keepdims=True)
    p = jnp.where(causal, jnp.exp2(s - m), 0.0)
    acc_ref[...] = whole(wide(split(p), v, 1, 0))
    l = jnp.sum(p, axis=-1, keepdims=True)
    stat_ref[...] = whole(jnp.where(lane == 0, m, jnp.where(lane == 1, l, den)))


def attend_kernel(whole, halves, final, at, docs, q_ref, acc0_ref, stat_ref, *refs):
    count = whole + halves
    pieces, refs = refs[: whole + 2 * halves], refs[whole + 2 * halves :]
    if final:
        t_ref, sq_ref, flags, buf, sem, keys, values, qs, m_sc, l_sc, acc = refs
    else:
        acc_out, stat_out, flags, buf, sem, keys, values, qs, m_sc, l_sc, acc = refs
    g = pl.program_id(0)
    head = g // (GRP // WIDE)

    def copies(k):
        if k < whole:
            return [pltpu.make_async_copy(pieces[k], buf.at[k], sem.at[k, 0])]
        pair = pieces[whole + 2 * (k - whole) : whole + 2 * (k - whole) + 2]
        return [pltpu.make_async_copy(pair[h], buf.at[k, h], sem.at[k, h]) for h in range(KVH)]

    @pl.when(g == 0)
    def _():
        note_wanted(docs, flags, range(at, at + count))
        for k in range(count):

            @pl.when(flags[k] == 1)
            def _(k=k):
                for copy in copies(k):
                    copy.start()

    rows = TILE * TOK
    tiles = WIDE // TILE
    lane = lax.broadcasted_iota(jnp.int32, (rows, WID), 1)

    def take_up(i, carry):
        here = pl.ds(pl.multiple_of(i * rows, rows), rows)
        some = pl.ds(i * TILE, TILE)
        hi, lo = split(q_ref[some].reshape(rows, WID) * (LOG2E / math.sqrt(WID)))
        qs[here, :WID] = hi
        qs[here, WID:] = lo
        stat = stat_ref[some].reshape(rows, WID)
        m_sc[here, :] = jnp.broadcast_to(stat[:, 0:1], (rows, WID))
        l_sc[here, :] = jnp.where(lane == 1, stat, 0.0)
        acc[here, :] = acc0_ref[some].reshape(rows, WID)
        return carry

    lax.fori_loop(0, tiles, take_up, 0)

    @pl.when(g == 0)
    def _():
        for k in range(count):

            @pl.when(flags[k] == 1)
            def _(k=k):
                for copy in copies(k):
                    copy.wait()

        def divide(n, carry):
            k, h = n // KVH, n % KVH
            keys[k, h, :, :WID], keys[k, h, :, WID:] = split(buf[k, h, 0])
            values[k, h, :, :WID], values[k, h, :, WID:] = split(buf[k, h, 1])
            return carry

        lax.fori_loop(0, count * KVH, divide, 0)

    def visit(k, carry):
        @pl.when(flags[k] == 1)
        def _():
            kh, kl = keys[k, head, :, :WID], keys[k, head, :, WID:]
            v_both = values[k, head]
            k_twice = jnp.concatenate([kh, kh], 1)
            for i in range(tiles):
                here = pl.ds(i * rows, rows)
                q = qs[here, :]
                s = dot(q, k_twice, 1, 1) + dot(q[:, :WID], kl, 1, 1)
                m_old = m_sc[here, :]
                m_new = jnp.maximum(m_old, jnp.max(s, axis=-1, keepdims=True))
                p = jnp.exp2(s - jnp.concatenate([m_new, m_new], 1))
                fade = jnp.exp2(m_old - m_new)
                m_sc[here, :] = m_new
                l_sc[here, :] = fade * l_sc[here, :] + p[:, :WID] + p[:, WID:]
                ph, pl_ = split(p)
                both = dot(ph, v_both, 1, 0)
                acc[here, :] = (
                    fade * acc[here, :] + both[:, :WID] + both[:, WID:] + dot(pl_, v_both[:, :WID], 1, 0)
                )

        return carry

    lax.fori_loop(0, count, visit, 0)
    if not final:

        def put_down(i, carry):
            here = pl.ds(pl.multiple_of(i * rows, rows), rows)
            some = pl.ds(i * TILE, TILE)
            acc_out[some] = acc[here, :].reshape(TILE, TOK, WID)
            l = jnp.sum(l_sc[here, :], axis=-1, keepdims=True)
            stat = jnp.where(lane == 1, l, stat_ref[some].reshape(rows, WID))
            stat_out[some] = jnp.where(lane == 0, m_sc[here, :], stat).reshape(TILE, TOK, WID)
            return carry

        lax.fori_loop(0, tiles, put_down, 0)
        return
    total = jnp.zeros((TOK, WID), F32)
    for i in range(tiles):
        here = pl.ds(i * rows, rows)
        t = acc[here, :] / jnp.sum(l_sc[here, :], axis=-1, keepdims=True)
        t_ref[i * TILE : (i + 1) * TILE] = t.reshape(TILE, TOK, WID)
        for k in range(TILE):
            part = t[k * TOK : (k + 1) * TOK]
            total = total + part * part
    line = jnp.sum(total, axis=-1, keepdims=True)
    line = jnp.transpose(jnp.broadcast_to(line, (TOK, WID)))[:8]

    @pl.when(g == 0)
    def _():
        sq_ref[...] = line

    @pl.when(g > 0)
    def _():
        sq_ref[...] += line


def student_kernel(
    docs, q_ref, qf_ref, num_ref, stat_ref, a_ref, t_ref, w_ref, v_ref, kf_ref, states_ref,
    sq0_ref, sq1_ref, sq2_ref, sq3_ref, gq_ref, mq_ref, gkf_ref, gv_ref, s_ref, prior_ref, scale_ref, both_ref,
):
    step = pl.program_id(0)
    per = GRP // STEP

    @pl.when(step % per == 0)
    def _():
        gkf_ref[...] = jnp.zeros_like(gkf_ref)
        gv_ref[...] = jnp.zeros_like(gv_ref)
        s_ref[...] = jnp.zeros_like(s_ref)
        first, own, _ = bounds(docs)
        prior_ref[...] = lax.fori_loop(
            first, own, lambda j, held: held + states_ref[j, 0], jnp.zeros((SROWS, WID), F32)
        )

        both_ref[:, :WID] = prior_ref[:WID]
        both_ref[:, WID:] = jnp.transpose(jnp.broadcast_to(prior_ref[WID : WID + 1], (WID, WID)))

    @pl.when(step == 0)
    def _():
        squares = sq0_ref[...] + sq1_ref[...] + sq2_ref[...] + sq3_ref[...]
        mean = squares / (4 * HEADS * WID) + 1e-6
        scale_ref[...] = jnp.broadcast_to(jnp.transpose(2.0 / mean)[:, 0:1], (TOK, WID))

    both = split(both_ref[...])
    prior = both[0][:, :WID], both[1][:, :WID]
    prior_n = prior_ref[WID : WID + 1]
    v, kf = split(v_ref[0]), split(kf_ref[0])
    scale = jnp.concatenate([scale_ref[...]] * STEP, 0)
    rows = STEP * TOK
    causal = stacked_mask(STEP)
    flat = lambda ref: ref[...].reshape(rows, ref.shape[-1])
    qf = flat(qf_ref)
    qfs = split(qf)
    carried = deep(qfs, both, 1, 0)
    num = flat(num_ref) + carried[:, :WID]
    den = flat(stat_ref)[:, 2:3] + carried[:, WID:]
    inv = 1.0 / den
    student = num * inv
    gn = (student - flat(t_ref)) * (scale * inv)
    gd = -row_sum(gn * student)
    gns = split(gn)
    gs = jnp.where(causal, deep(gns, v, 1, 1) + jnp.concatenate([gd, gd], 1), 0.0)
    gss = split(gs)
    gqf = deep(gns, prior, 1, 1) + gd * prior_n + wide(gss, kf, 1, 0)
    qlg = qf * (gqf - row_sum(qf * gqf))
    qlh, qll = split(qlg)
    for i, at in enumerate(HEAD_ROWS[:STEP]):
        part = (qlh[at], qll[at])
        gq_ref[i] = deep(part, split(w_ref[i]), 1, 1)
        mq_ref[i] = wide(split(q_ref[i]), part, 0, 0)
    gkf_ref[0] += wide(gss, qfs, 0, 0)
    gv_ref[0] += wide(split(flat(a_ref)), gns, 0, 0)
    s_ref[0, :WID] += wide(qfs, gns, 0, 0)
    s_ref[0, WID:] += jnp.broadcast_to(jnp.sum(qf * gd, axis=0, keepdims=True), (8, WID))


def key_map_kernel(docs, k_ref, kf_ref, gkf_ref, s_ref, wk_ref, *refs):
    pieces, (mk_ref, flags, order, buf, sem) = refs[:-5], refs[-5:]
    note_wanted(docs, flags, (0, 1, 2, 3, 4, 5, 7, 8, 6, 9, 10))
    state = [split(s_ref[h, :WID]) for h in range(KVH)]
    norm = [s_ref[h, WID : WID + 1] for h in range(KVH)]
    wk = [split(wk_ref[h]) for h in range(KVH)]

    def copies(k):
        if k < 8:
            return [pltpu.make_async_copy(pieces[k], buf.at[k], sem.at[k, 0])]
        return [pltpu.make_async_copy(pieces[2 * k - 8 + h], buf.at[k, h], sem.at[k, h]) for h in range(KVH)]

    for k in range(11):

        @pl.when(flags[k] == 1)
        def _(k=k):
            for copy in copies(k):
                copy.start()

    def logit_grad(feats, grad):
        return feats * (grad - row_sum(feats * grad))

    for h in range(KVH):
        mk_ref[h] = wide(split(k_ref[h]), split(logit_grad(kf_ref[h], gkf_ref[h])), 0, 0)
    for k in range(11):

        @pl.when(flags[k] == 1)
        def _(k=k):
            for copy in copies(k):
                copy.wait()

    count = jnp.int32(0)
    for k in range(11):
        order[count] = k
        count = count + flags[k]

    def visit(n, carry):
        one = order[2 * n]
        full_pair = 2 * n + 1 < count
        two = jnp.where(full_pair, order[jnp.minimum(2 * n + 1, 11)], one)
        row = lax.broadcasted_iota(jnp.int32, (2 * TOK, WID), 0)
        kept = (row < TOK) | full_pair
        for h in range(KVH):
            ks = split(jnp.concatenate([buf[one, h, 0], buf[two, h, 0]], 0))
            vs = split(jnp.concatenate([buf[one, h, 1], buf[two, h, 1]], 0))
            feats = softmax(deep(ks, wk[h], 1, 0))
            grad = deep(vs, state[h], 1, 1) + norm[h]
            mk_ref[h] += wide(ks, split(jnp.where(kept, logit_grad(feats, grad), 0.0)), 0, 0)
        return carry

    lax.fori_loop(0, (count + 1) // 2, visit, 0)


def later_kernel(docs, s_ref, gkf_ref, gv_ref, kf_ref, v_ref, wk_ref, gk_ref, out_ref):
    _, own, last = bounds(docs)
    for h in range(KVH):
        total = lax.fori_loop(
            own + 1, last + 1, lambda j, held: held + s_ref[j, h], jnp.zeros((SROWS, WID), F32)
        )
        state, norm = split(total[:WID]), total[WID : WID + 1]
        kf = kf_ref[h]
        gkf = gkf_ref[h] + deep(split(v_ref[h]), state, 1, 1) + norm
        out_ref[h] = gv_ref[h] + deep(split(kf), state, 1, 0)
        klg = kf * (gkf - row_sum(kf * gkf))
        gk_ref[h] = deep(split(klg), split(wk_ref[h]), 1, 1)


def shape(*dims):
    return jax.ShapeDtypeStruct(dims, F32)


def full(*dims):
    return pl.BlockSpec(dims, lambda *_: (0,) * len(dims))


def params(limit=56):
    return pltpu.CompilerParams(vmem_limit_bytes=limit * 1024 * 1024)


def cost(us):
    return pl.CostEstimate(flops=int(us * 1e9), bytes_accessed=int(us * 3e5), transcendentals=0)


def body(queries, key_rows, value_rows, query_map, key_map, block_doc):
    keys = jnp.transpose(key_rows[0], (1, 0, 2))
    values = jnp.transpose(value_rows[0], (1, 0, 2))
    mine = jnp.stack([keys, values], 1)
    down = lambda x: lax.ppermute(x, "ctx_0", [(i, i + 1) for i in range(3)])
    right = lambda x: lax.ppermute(x, "ctx_1", [(i, (i + 1) % 4) for i in range(4)])
    left = lambda x: lax.ppermute(x, "ctx_1", [(i, (i - 1) % 4) for i in range(4)])
    docs = block_doc[0]
    q = jnp.transpose(queries[0], (1, 0, 2))
    per = GRP // STEP
    by_head = lambda *dims: pl.BlockSpec((STEP, *dims), lambda g, *_: (g, 0, 0))
    by_kv = lambda *dims: pl.BlockSpec((1, *dims), lambda g, *_: (g // per, 0, 0))

    any_spec = pl.BlockSpec(memory_space=pl.ANY)

    def local(h, held):
        part = lambda *dims: pl.BlockSpec((EARLY, *dims), lambda g: (g + h * (GRP // EARLY), 0, 0))
        kv = lambda *dims: pl.BlockSpec((1, *dims), lambda g: (h, 0, 0))
        return pl.pallas_call(
            local_kernel,
            grid=(GRP // EARLY,),
            in_specs=[part(TOK, WID), kv(TOK, WID), kv(TOK, WID), part(WID, WID), kv(WID, WID)]
            + [any_spec] * len(held),
            out_specs=[part(TOK, WID)] * 4 + [part(TOK, TOK), kv(TOK, WID), kv(SROWS, WID)],
            out_shape=[shape(HEADS, TOK, WID)] * 4
            + [shape(HEADS, TOK, TOK), shape(KVH, TOK, WID), shape(KVH, SROWS, WID)],
            input_output_aliases={5 + i: i for i in range(len(held))},
            compiler_params=params(),
            cost_estimate=cost(8),
            name="local",
        )(q, keys, values, query_map, key_map, *held)

    arrived = down(mine), right(mine), left(mine)
    held = local(0, ())
    (za, yp0, ym0), held = lax.optimization_barrier((arrived, held))
    zb, yp1, ym1 = down(za), right(za), left(za)
    yp2, ym2 = right(zb), left(zb)
    across = [(right(p[0]), left(m[1])) for p, m in ((yp0, ym0), (yp1, ym1), (yp2, ym2))]

    qf, num, acc, stat, a, kf, states = local(1, held)
    block_states = lax.all_gather(states, CTX)

    wide_head = lambda *dims: pl.BlockSpec((WIDE, *dims), lambda g, *_: (g, 0, 0))

    def attend(acc, stat, whole, halves, at, final, us):
        count = len(whole) + len(halves)
        return pl.pallas_call(
            functools.partial(attend_kernel, len(whole), len(halves), final, at),
            grid_spec=pltpu.PrefetchScalarGridSpec(
                num_scalar_prefetch=1,
                grid=(HEADS // WIDE,),
                in_specs=[wide_head(TOK, WID)] * 3 + [any_spec] * (len(whole) + 2 * len(halves)),
                out_specs=[wide_head(TOK, WID), full(8, TOK) if final else wide_head(TOK, WID)],
                scratch_shapes=[
                    pltpu.SMEM((count,), jnp.int32),
                    pltpu.VMEM((count, KVH, 2, TOK, WID), F32),
                    pltpu.SemaphoreType.DMA((count, KVH)),
                    pltpu.VMEM((count, KVH, TOK, 2 * WID), BF16),
                    pltpu.VMEM((count, KVH, TOK, 2 * WID), BF16),
                    pltpu.VMEM((WIDE * TOK, 2 * WID), BF16),
                ]
                + [pltpu.VMEM((WIDE * TOK, WID), F32)] * 3,
            ),
            out_shape=[shape(HEADS, TOK, WID), shape(8, TOK) if final else shape(HEADS, TOK, WID)],
            compiler_params=params(26),
            cost_estimate=cost(us),
            name="attend",
        )(docs, q, acc, stat, *whole, *[x for pair in halves for x in pair])

    acc, stat = attend(acc, stat, [yp0, ym0, za], [], 0, False, 14)
    acc, stat = attend(acc, stat, [yp1, ym1, zb], [across[0]], 3, False, 16)
    acc, stat = attend(acc, stat, [yp2, ym2], [across[1]], 7, False, 12)
    teacher, squares = attend(acc, stat, [], [across[2]], 10, True, 6)
    others = [lax.ppermute(squares, "head", [(i, (i + k) % 4) for i in range(4)]) for k in (1, 2, 3)]

    gq, mq, gkf, gv, states = pl.pallas_call(
        student_kernel,
        grid_spec=pltpu.PrefetchScalarGridSpec(
            num_scalar_prefetch=1,
            grid=(HEADS // STEP,),
            in_specs=[
                by_head(TOK, WID), by_head(TOK, WID), by_head(TOK, WID), by_head(TOK, WID), by_head(TOK, TOK),
                by_head(TOK, WID), by_head(WID, WID), by_kv(TOK, WID), by_kv(TOK, WID),
                pl.BlockSpec((N_CTX, 1, SROWS, WID), lambda g, *_: (0, g // per, 0, 0)),
                full(8, TOK), full(8, TOK), full(8, TOK), full(8, TOK),
            ],
            out_specs=[by_head(TOK, WID), by_head(WID, WID), by_kv(TOK, WID), by_kv(TOK, WID), by_kv(SROWS, WID)],
            scratch_shapes=[
                pltpu.VMEM((SROWS, WID), F32), pltpu.VMEM((TOK, WID), F32), pltpu.VMEM((WID, 2 * WID), F32),
            ],
        ),
        out_shape=[
            shape(HEADS, TOK, WID), shape(HEADS, WID, WID), shape(KVH, TOK, WID), shape(KVH, TOK, WID),
            shape(KVH, SROWS, WID),
        ],
        compiler_params=params(),
        cost_estimate=cost(25),
        name="student",
    )(docs, q, qf, num, stat, a, teacher, query_map, values, kf, block_states, squares, *others)

    all_states = lax.all_gather(states, CTX)
    share = lambda x: jnp.sum(lax.all_to_all(x.reshape(32, -1, WID), DP_CTX, 0, 0, tiled=True), axis=0)
    query_part = share(mq)
    mk = pl.pallas_call(
        key_map_kernel,
        grid_spec=pltpu.PrefetchScalarGridSpec(
            num_scalar_prefetch=1,
            grid=(1,),
            in_specs=[full(KVH, TOK, WID)] * 3 + [full(KVH, SROWS, WID), full(KVH, WID, WID)] + [any_spec] * 14,
            out_specs=full(KVH, WID, WID),
            scratch_shapes=[pltpu.SMEM((11,), jnp.int32), pltpu.SMEM((12,), jnp.int32), pltpu.VMEM((11, KVH, 2, TOK, WID), F32), pltpu.SemaphoreType.DMA((11, KVH))],
        ),
        out_shape=shape(KVH, WID, WID),
        compiler_params=params(),
        cost_estimate=cost(10),
        name="key_map",
    )(docs, keys, kf, gkf, states, key_map,
      yp0, ym0, za, yp1, ym1, zb, yp2, ym2, *[x for pair in across for x in pair])
    mk, query_part = lax.optimization_barrier((mk, query_part))
    parts = jnp.concatenate([query_part, share(mk)])
    maps = lax.all_to_all(jnp.broadcast_to(parts, (32, *parts.shape)), DP_CTX, 0, 0, tiled=True)
    rows = HEADS * WID // 32
    grad_keys, grad_values = pl.pallas_call(
        later_kernel,
        grid_spec=pltpu.PrefetchScalarGridSpec(
            num_scalar_prefetch=1,
            grid=(1,),
            in_specs=[full(N_CTX, KVH, SROWS, WID)] + [full(KVH, TOK, WID)] * 4 + [full(KVH, WID, WID)],
            out_specs=[full(KVH, TOK, WID)] * 2,
        ),
        out_shape=[shape(KVH, TOK, WID)] * 2,
        compiler_params=params(),
        name="later",
    )(docs, all_states, gkf, gv, kf, values, key_map)
    back = lambda x: jnp.transpose(x, (1, 0, 2))[None]
    return (back(gq), back(grad_keys), back(grad_values), maps[:, :rows].reshape(mq.shape), maps[:, rows:].reshape(mk.shape))


def solution(mesh):
    torus = Mesh(
        mesh.devices.reshape(mesh.shape["dp"], 4, 4, mesh.shape["head"]),
        ("dp", "ctx_0", "ctx_1", "head"),
    )
    rows = P("dp", CTX, "head", None)
    placed = (rows, rows, rows, P("head", None, None), P("head", None, None), P("dp", None))
    return jax.shard_map(
        body, mesh=torus, in_specs=placed, out_specs=(rows, rows, rows, placed[3], placed[4]), check_vma=False
    )
```

```python
import functools
import math

import jax
import jax.numpy as jnp
from jax import lax
from jax.experimental import pallas as pl
from jax.experimental.pallas import tpu as pltpu
from jax.sharding import Mesh
from jax.sharding import PartitionSpec as P


CTX = ("ctx_0", "ctx_1")
DP_CTX = ("dp", "ctx_0", "ctx_1")
F32 = jnp.float32
BF16 = jnp.bfloat16
LOG2E = 1.0 / math.log(2.0)
TOK = 256
WID = 128
GRP = 8
KVH = 2
HEADS = GRP * KVH
STEP = 4
EARLY = 4
WIDE = 8
TILE = 1
N_CTX = 16
SROWS = WID + 8


def split(x):
    hi = x.astype(BF16)
    return hi, (x - hi.astype(F32)).astype(BF16)


def dot(a, b, ca, cb):
    return lax.dot_general(a, b, (((ca,), (cb,)), ((), ())), preferred_element_type=F32)


def deep(a, b, ca, cb):
    ah, al = a
    bh, bl = b
    return dot(jnp.concatenate([ah, al], ca), jnp.concatenate([bh, bh], cb), ca, cb) + dot(ah, bl, ca, cb)


def wide(a, b, ca, cb):
    ah, al = a
    bh, bl = b
    n = bh.shape[1 - cb]
    both = dot(ah, jnp.concatenate([bh, bl], 1 - cb), ca, cb)
    return both[:, :n] + both[:, n:] + dot(al, bh, ca, cb)


def softmax(x):
    e = jnp.exp(x - jnp.max(x, axis=-1, keepdims=True))
    return e / row_sum(e)


SOURCES = ((0, 3), (0, 1), (1, 0), (0, 2), (1, 3), (1, 1), (2, 0), (2, 3), (2, 1), (1, 2), (2, 2))


def bounds(docs):
    own = 4 * lax.axis_index("ctx_0") + lax.axis_index("ctx_1")
    first, last = 0, -1
    for j in range(N_CTX):
        first = first + (docs[j] < docs[own]).astype(jnp.int32)
        last = last + (docs[j] <= docs[own]).astype(jnp.int32)
    return first, own, last


def note_wanted(docs, flags, places):
    row, column = lax.axis_index("ctx_0"), lax.axis_index("ctx_1")
    own = 4 * row + column
    for k, place in enumerate(places):
        back, on = SOURCES[place]
        source = 4 * (row - back) + lax.rem(column + on, 4)
        seen = (source >= 0) & (source < own)
        flags[k] = (seen & (docs[jnp.maximum(source, 0)] == docs[own])).astype(jnp.int32)


HEAD_ROWS = [slice(i * TOK, (i + 1) * TOK) for i in range(GRP)]


def stacked_mask(heads):
    row = lax.broadcasted_iota(jnp.int32, (heads * TOK, TOK), 0)
    return lax.rem(row, TOK) >= lax.broadcasted_iota(jnp.int32, (heads * TOK, TOK), 1)


def row_sum(x):
    return dot(jnp.concatenate(split(x), 1), jnp.ones((2 * WID, WID), BF16), 1, 0)


def local_kernel(q_ref, k_ref, v_ref, w_ref, wk_ref, *refs):
    qf_ref, num_ref, acc_ref, stat_ref, a_ref, kf_ref, s_ref = refs[-7:]

    @pl.when(pl.program_id(0) == 0)
    def _():
        kf = softmax(deep(split(k_ref[0]), split(wk_ref[0]), 1, 0))
        kf_ref[0] = kf
        s_ref[0, :WID] = wide(split(kf), split(v_ref[0]), 0, 0)
        s_ref[0, WID:] = jnp.broadcast_to(jnp.sum(kf, axis=0, keepdims=True), (8, WID))

    k, v, kf = split(k_ref[0]), split(v_ref[0]), split(kf_ref[0])
    rows = EARLY * TOK
    causal = stacked_mask(EARLY)
    lane = lax.broadcasted_iota(jnp.int32, (rows, WID), 1)
    whole = lambda x: x.reshape(EARLY, TOK, x.shape[-1])
    q = q_ref[...].reshape(rows, WID)
    qh, ql = split(q)
    logits = [deep((qh[at], ql[at]), split(w_ref[i]), 1, 0) for i, at in enumerate(HEAD_ROWS[:EARLY])]
    qf = softmax(jnp.concatenate(logits, 0))
    qf_ref[...] = whole(qf)
    a = jnp.where(causal, deep(split(qf), kf, 1, 1), 0.0)
    a_ref[...] = whole(a)
    num_ref[...] = whole(wide(split(a), v, 1, 0))
    den = jnp.sum(a, axis=-1, keepdims=True)
    s = deep(split(q * (LOG2E / math.sqrt(WID))), k, 1, 1)
    s = jnp.where(causal, s, -1e30)
    m = jnp.max(s, axis=-1, keepdims=True)
    p = jnp.where(causal, jnp.exp2(s - m), 0.0)
    acc_ref[...] = whole(wide(split(p), v, 1, 0))
    l = jnp.sum(p, axis=-1, keepdims=True)
    stat_ref[...] = whole(jnp.where(lane == 0, m, jnp.where(lane == 1, l, den)))


def attend_kernel(whole, halves, final, at, docs, q_ref, acc0_ref, stat_ref, *refs):
    count = whole + halves
    pieces, refs = refs[: whole + 2 * halves], refs[whole + 2 * halves :]
    if final:
        t_ref, sq_ref, flags, buf, sem, keys, values, qs, m_sc, l_sc, acc = refs
    else:
        acc_out, stat_out, flags, buf, sem, keys, values, qs, m_sc, l_sc, acc = refs
    g = pl.program_id(0)
    head = g // (GRP // WIDE)

    def copies(k):
        if k < whole:
            return [pltpu.make_async_copy(pieces[k], buf.at[k], sem.at[k, 0])]
        pair = pieces[whole + 2 * (k - whole) : whole + 2 * (k - whole) + 2]
        return [pltpu.make_async_copy(pair[h], buf.at[k, h], sem.at[k, h]) for h in range(KVH)]

    @pl.when(g == 0)
    def _():
        note_wanted(docs, flags, range(at, at + count))
        for k in range(count):

            @pl.when(flags[k] == 1)
            def _(k=k):
                for copy in copies(k):
                    copy.start()

    rows = TILE * TOK
    tiles = WIDE // TILE
    lane = lax.broadcasted_iota(jnp.int32, (rows, WID), 1)

    def take_up(i, carry):
        here = pl.ds(pl.multiple_of(i * rows, rows), rows)
        some = pl.ds(i * TILE, TILE)
        hi, lo = split(q_ref[some].reshape(rows, WID) * (LOG2E / math.sqrt(WID)))
        qs[here, :WID] = hi
        qs[here, WID:] = lo
        stat = stat_ref[some].reshape(rows, WID)
        m_sc[here, :] = jnp.broadcast_to(stat[:, 0:1], (rows, WID))
        l_sc[here, :] = jnp.where(lane == 1, stat, 0.0)
        acc[here, :] = acc0_ref[some].reshape(rows, WID)
        return carry

    lax.fori_loop(0, tiles, take_up, 0, unroll=True)

    @pl.when(g == 0)
    def _():
        for k in range(count):

            @pl.when(flags[k] == 1)
            def _(k=k):
                for copy in copies(k):
                    copy.wait()

        def divide(n, carry):
            k, h = n // KVH, n % KVH
            keys[k, h, :, :WID], keys[k, h, :, WID:] = split(buf[k, h, 0])
            values[k, h, :, :WID], values[k, h, :, WID:] = split(buf[k, h, 1])
            return carry

        lax.fori_loop(0, count * KVH, divide, 0)

    def visit(k, carry):
        @pl.when(flags[k] == 1)
        def _():
            kh, kl = keys[k, head, :, :WID], keys[k, head, :, WID:]
            v_both = values[k, head]
            k_twice = jnp.concatenate([kh, kh], 1)
            for i in range(tiles):
                here = pl.ds(i * rows, rows)
                q = qs[here, :]
                s = dot(q, k_twice, 1, 1) + dot(q[:, :WID], kl, 1, 1)
                m_old = m_sc[here, :]
                m_new = jnp.maximum(m_old, jnp.max(s, axis=-1, keepdims=True))
                p = jnp.exp2(s - jnp.concatenate([m_new, m_new], 1))
                fade = jnp.exp2(m_old - m_new)
                m_sc[here, :] = m_new
                l_sc[here, :] = fade * l_sc[here, :] + p[:, :WID] + p[:, WID:]
                ph, pl_ = split(p)
                both = dot(ph, v_both, 1, 0)
                acc[here, :] = (
                    fade * acc[here, :] + both[:, :WID] + both[:, WID:] + dot(pl_, v_both[:, :WID], 1, 0)
                )

        return carry

    lax.fori_loop(0, count, visit, 0)
    if not final:

        def put_down(i, carry):
            here = pl.ds(pl.multiple_of(i * rows, rows), rows)
            some = pl.ds(i * TILE, TILE)
            acc_out[some] = acc[here, :].reshape(TILE, TOK, WID)
            l = jnp.sum(l_sc[here, :], axis=-1, keepdims=True)
            stat = jnp.where(lane == 1, l, stat_ref[some].reshape(rows, WID))
            stat_out[some] = jnp.where(lane == 0, m_sc[here, :], stat).reshape(TILE, TOK, WID)
            return carry

        lax.fori_loop(0, tiles, put_down, 0, unroll=True)
        return
    total = jnp.zeros((TOK, WID), F32)
    for i in range(tiles):
        here = pl.ds(i * rows, rows)
        t = acc[here, :] / jnp.sum(l_sc[here, :], axis=-1, keepdims=True)
        t_ref[i * TILE : (i + 1) * TILE] = t.reshape(TILE, TOK, WID)
        for k in range(TILE):
            part = t[k * TOK : (k + 1) * TOK]
            total = total + part * part
    line = jnp.sum(total, axis=-1, keepdims=True)
    line = jnp.transpose(jnp.broadcast_to(line, (TOK, WID)))[:8]

    @pl.when(g == 0)
    def _():
        sq_ref[...] = line

    @pl.when(g > 0)
    def _():
        sq_ref[...] += line


def student_kernel(
    docs, q_ref, qf_ref, num_ref, stat_ref, a_ref, t_ref, w_ref, v_ref, kf_ref, states_ref,
    sq0_ref, sq1_ref, sq2_ref, sq3_ref, gq_ref, mq_ref, gkf_ref, gv_ref, s_ref, prior_ref, scale_ref, both_ref,
):
    step = pl.program_id(0)
    per = GRP // STEP

    @pl.when(step % per == 0)
    def _():
        gkf_ref[...] = jnp.zeros_like(gkf_ref)
        gv_ref[...] = jnp.zeros_like(gv_ref)
        s_ref[...] = jnp.zeros_like(s_ref)
        first, own, _ = bounds(docs)
        prior_ref[...] = lax.fori_loop(
            first, own, lambda j, held: held + states_ref[j, 0], jnp.zeros((SROWS, WID), F32)
        )

        both_ref[:, :WID] = prior_ref[:WID]
        both_ref[:, WID:] = jnp.transpose(jnp.broadcast_to(prior_ref[WID : WID + 1], (WID, WID)))

    @pl.when(step == 0)
    def _():
        squares = sq0_ref[...] + sq1_ref[...] + sq2_ref[...] + sq3_ref[...]
        mean = squares / (4 * HEADS * WID) + 1e-6
        scale_ref[...] = jnp.broadcast_to(jnp.transpose(2.0 / mean)[:, 0:1], (TOK, WID))

    both = split(both_ref[...])
    prior = both[0][:, :WID], both[1][:, :WID]
    prior_n = prior_ref[WID : WID + 1]
    v, kf = split(v_ref[0]), split(kf_ref[0])
    scale = jnp.concatenate([scale_ref[...]] * STEP, 0)
    rows = STEP * TOK
    causal = stacked_mask(STEP)
    flat = lambda ref: ref[...].reshape(rows, ref.shape[-1])
    qf = flat(qf_ref)
    qfs = split(qf)
    carried = deep(qfs, both, 1, 0)
    num = flat(num_ref) + carried[:, :WID]
    den = flat(stat_ref)[:, 2:3] + carried[:, WID:]
    inv = 1.0 / den
    student = num * inv
    gn = (student - flat(t_ref)) * (scale * inv)
    gd = -row_sum(gn * student)
    gns = split(gn)
    gs = jnp.where(causal, deep(gns, v, 1, 1) + jnp.concatenate([gd, gd], 1), 0.0)
    gss = split(gs)
    gqf = deep(gns, prior, 1, 1) + gd * prior_n + wide(gss, kf, 1, 0)
    qlg = qf * (gqf - row_sum(qf * gqf))
    qlh, qll = split(qlg)
    for i, at in enumerate(HEAD_ROWS[:STEP]):
        part = (qlh[at], qll[at])
        gq_ref[i] = deep(part, split(w_ref[i]), 1, 1)
        mq_ref[i] = wide(split(q_ref[i]), part, 0, 0)
    gkf_ref[0] += wide(gss, qfs, 0, 0)
    gv_ref[0] += wide(split(flat(a_ref)), gns, 0, 0)
    s_ref[0, :WID] += wide(qfs, gns, 0, 0)
    s_ref[0, WID:] += jnp.broadcast_to(jnp.sum(qf * gd, axis=0, keepdims=True), (8, WID))


def key_map_kernel(docs, k_ref, kf_ref, gkf_ref, s_ref, wk_ref, *refs):
    pieces, (mk_ref, flags, order, buf, sem) = refs[:-5], refs[-5:]
    note_wanted(docs, flags, (0, 1, 2, 4, 5, 6, 7, 8, 3, 9, 10))
    state = [split(s_ref[h, :WID]) for h in range(KVH)]
    norm = [s_ref[h, WID : WID + 1] for h in range(KVH)]
    wk = [split(wk_ref[h]) for h in range(KVH)]

    def copies(k):
        if k < 8:
            return [pltpu.make_async_copy(pieces[k], buf.at[k], sem.at[k, 0])]
        return [pltpu.make_async_copy(pieces[2 * k - 8 + h], buf.at[k, h], sem.at[k, h]) for h in range(KVH)]

    for k in range(11):

        @pl.when(flags[k] == 1)
        def _(k=k):
            for copy in copies(k):
                copy.start()

    def logit_grad(feats, grad):
        return feats * (grad - row_sum(feats * grad))

    for h in range(KVH):
        mk_ref[h] = wide(split(k_ref[h]), split(logit_grad(kf_ref[h], gkf_ref[h])), 0, 0)
    for k in range(11):

        @pl.when(flags[k] == 1)
        def _(k=k):
            for copy in copies(k):
                copy.wait()

    count = jnp.int32(0)
    for k in range(11):
        order[count] = k
        count = count + flags[k]

    def visit(n, carry):
        one = order[2 * n]
        full_pair = 2 * n + 1 < count
        two = jnp.where(full_pair, order[jnp.minimum(2 * n + 1, 11)], one)
        row = lax.broadcasted_iota(jnp.int32, (2 * TOK, WID), 0)
        kept = (row < TOK) | full_pair
        for h in range(KVH):
            ks = split(jnp.concatenate([buf[one, h, 0], buf[two, h, 0]], 0))
            vs = split(jnp.concatenate([buf[one, h, 1], buf[two, h, 1]], 0))
            feats = softmax(deep(ks, wk[h], 1, 0))
            grad = deep(vs, state[h], 1, 1) + norm[h]
            mk_ref[h] += wide(ks, split(jnp.where(kept, logit_grad(feats, grad), 0.0)), 0, 0)
        return carry

    lax.fori_loop(0, (count + 1) // 2, visit, 0)


def later_kernel(docs, s_ref, gkf_ref, gv_ref, kf_ref, v_ref, wk_ref, gk_ref, out_ref):
    _, own, last = bounds(docs)
    for h in range(KVH):
        total = lax.fori_loop(
            own + 1, last + 1, lambda j, held: held + s_ref[j, h], jnp.zeros((SROWS, WID), F32)
        )
        state, norm = split(total[:WID]), total[WID : WID + 1]
        kf = kf_ref[h]
        gkf = gkf_ref[h] + deep(split(v_ref[h]), state, 1, 1) + norm
        out_ref[h] = gv_ref[h] + deep(split(kf), state, 1, 0)
        klg = kf * (gkf - row_sum(kf * gkf))
        gk_ref[h] = deep(split(klg), split(wk_ref[h]), 1, 1)


def shape(*dims):
    return jax.ShapeDtypeStruct(dims, F32)


def full(*dims):
    return pl.BlockSpec(dims, lambda *_: (0,) * len(dims))


def params(limit=56):
    return pltpu.CompilerParams(vmem_limit_bytes=limit * 1024 * 1024)


def cost(us):
    return pl.CostEstimate(flops=int(us * 1e9), bytes_accessed=int(us * 3e5), transcendentals=0)


def body(queries, key_rows, value_rows, query_map, key_map, block_doc):
    keys = jnp.transpose(key_rows[0], (1, 0, 2))
    values = jnp.transpose(value_rows[0], (1, 0, 2))
    mine = jnp.stack([keys, values], 1)
    down = lambda x: lax.ppermute(x, "ctx_0", [(i, i + 1) for i in range(3)])
    right = lambda x: lax.ppermute(x, "ctx_1", [(i, (i + 1) % 4) for i in range(4)])
    left = lambda x: lax.ppermute(x, "ctx_1", [(i, (i - 1) % 4) for i in range(4)])
    docs = block_doc[0]
    q = jnp.transpose(queries[0], (1, 0, 2))
    per = GRP // STEP
    by_head = lambda *dims: pl.BlockSpec((STEP, *dims), lambda g, *_: (g, 0, 0))
    by_kv = lambda *dims: pl.BlockSpec((1, *dims), lambda g, *_: (g // per, 0, 0))

    any_spec = pl.BlockSpec(memory_space=pl.ANY)

    def local(h, held):
        part = lambda *dims: pl.BlockSpec((EARLY, *dims), lambda g: (g + h * (GRP // EARLY), 0, 0))
        kv = lambda *dims: pl.BlockSpec((1, *dims), lambda g: (h, 0, 0))
        return pl.pallas_call(
            local_kernel,
            grid=(GRP // EARLY,),
            in_specs=[part(TOK, WID), kv(TOK, WID), kv(TOK, WID), part(WID, WID), kv(WID, WID)]
            + [any_spec] * len(held),
            out_specs=[part(TOK, WID)] * 4 + [part(TOK, TOK), kv(TOK, WID), kv(SROWS, WID)],
            out_shape=[shape(HEADS, TOK, WID)] * 4
            + [shape(HEADS, TOK, TOK), shape(KVH, TOK, WID), shape(KVH, SROWS, WID)],
            input_output_aliases={5 + i: i for i in range(len(held))},
            compiler_params=params(),
            cost_estimate=cost(8),
            name="local",
        )(q, keys, values, query_map, key_map, *held)

    arrived = down(mine), right(mine), left(mine)
    held = local(0, ())
    (za, yp0, ym0), held = lax.optimization_barrier((arrived, held))
    cross = lambda p, m: (right(p[0]), left(m[1]))
    zb, yp1, ym1 = down(za), right(za), left(za)
    across = [cross(yp0, ym0)]
    yp2, ym2 = right(zb), left(zb)
    across.append(cross(yp1, ym1))
    across.append(cross(yp2, ym2))

    qf, num, acc, stat, a, kf, states = local(1, held)
    block_states = lax.all_gather(states, CTX)

    wide_head = lambda *dims: pl.BlockSpec((WIDE, *dims), lambda g, *_: (g, 0, 0))

    def attend(acc, stat, whole, halves, at, final, us):
        count = len(whole) + len(halves)
        return pl.pallas_call(
            functools.partial(attend_kernel, len(whole), len(halves), final, at),
            grid_spec=pltpu.PrefetchScalarGridSpec(
                num_scalar_prefetch=1,
                grid=(HEADS // WIDE,),
                in_specs=[wide_head(TOK, WID)] * 3 + [any_spec] * (len(whole) + 2 * len(halves)),
                out_specs=[wide_head(TOK, WID), full(8, TOK) if final else wide_head(TOK, WID)],
                scratch_shapes=[
                    pltpu.SMEM((count,), jnp.int32),
                    pltpu.VMEM((count, KVH, 2, TOK, WID), F32),
                    pltpu.SemaphoreType.DMA((count, KVH)),
                    pltpu.VMEM((count, KVH, TOK, 2 * WID), BF16),
                    pltpu.VMEM((count, KVH, TOK, 2 * WID), BF16),
                    pltpu.VMEM((WIDE * TOK, 2 * WID), BF16),
                ]
                + [pltpu.VMEM((WIDE * TOK, WID), F32)] * 3,
            ),
            out_shape=[shape(HEADS, TOK, WID), shape(8, TOK) if final else shape(HEADS, TOK, WID)],
            compiler_params=params(26),
            cost_estimate=cost(us),
            name="attend",
        )(docs, q, acc, stat, *whole, *[x for pair in halves for x in pair])

    acc, stat = attend(acc, stat, [yp0, ym0, za], [across[0]], 0, False, 16)
    acc, stat = attend(acc, stat, [yp1, ym1, zb, yp2, ym2], [across[1]], 4, False, 22)
    teacher, squares = attend(acc, stat, [], [across[2]], 10, True, 6)
    others = [lax.ppermute(squares, "head", [(i, (i + k) % 4) for i in range(4)]) for k in (1, 2, 3)]

    gq, mq, gkf, gv, states = pl.pallas_call(
        student_kernel,
        grid_spec=pltpu.PrefetchScalarGridSpec(
            num_scalar_prefetch=1,
            grid=(HEADS // STEP,),
            in_specs=[
                by_head(TOK, WID), by_head(TOK, WID), by_head(TOK, WID), by_head(TOK, WID), by_head(TOK, TOK),
                by_head(TOK, WID), by_head(WID, WID), by_kv(TOK, WID), by_kv(TOK, WID),
                pl.BlockSpec((N_CTX, 1, SROWS, WID), lambda g, *_: (0, g // per, 0, 0)),
                full(8, TOK), full(8, TOK), full(8, TOK), full(8, TOK),
            ],
            out_specs=[by_head(TOK, WID), by_head(WID, WID), by_kv(TOK, WID), by_kv(TOK, WID), by_kv(SROWS, WID)],
            scratch_shapes=[
                pltpu.VMEM((SROWS, WID), F32), pltpu.VMEM((TOK, WID), F32), pltpu.VMEM((WID, 2 * WID), F32),
            ],
        ),
        out_shape=[
            shape(HEADS, TOK, WID), shape(HEADS, WID, WID), shape(KVH, TOK, WID), shape(KVH, TOK, WID),
            shape(KVH, SROWS, WID),
        ],
        compiler_params=params(),
        cost_estimate=cost(25),
        name="student",
    )(docs, q, qf, num, stat, a, teacher, query_map, values, kf, block_states, squares, *others)

    all_states = lax.all_gather(states, CTX)
    share = lambda x: jnp.sum(lax.all_to_all(x.reshape(32, -1, WID), DP_CTX, 0, 0, tiled=True), axis=0)
    query_part = share(mq)
    mk = pl.pallas_call(
        key_map_kernel,
        grid_spec=pltpu.PrefetchScalarGridSpec(
            num_scalar_prefetch=1,
            grid=(1,),
            in_specs=[full(KVH, TOK, WID)] * 3 + [full(KVH, SROWS, WID), full(KVH, WID, WID)] + [any_spec] * 14,
            out_specs=full(KVH, WID, WID),
            scratch_shapes=[pltpu.SMEM((11,), jnp.int32), pltpu.SMEM((12,), jnp.int32), pltpu.VMEM((11, KVH, 2, TOK, WID), F32), pltpu.SemaphoreType.DMA((11, KVH))],
        ),
        out_shape=shape(KVH, WID, WID),
        compiler_params=params(),
        cost_estimate=cost(10),
        name="key_map",
    )(docs, keys, kf, gkf, states, key_map,
      yp0, ym0, za, yp1, ym1, zb, yp2, ym2, *[x for pair in across for x in pair])
    mk, query_part = lax.optimization_barrier((mk, query_part))
    parts = jnp.concatenate([query_part, share(mk)])
    maps = lax.all_to_all(jnp.broadcast_to(parts, (32, *parts.shape)), DP_CTX, 0, 0, tiled=True)
    rows = HEADS * WID // 32
    grad_keys, grad_values = pl.pallas_call(
        later_kernel,
        grid_spec=pltpu.PrefetchScalarGridSpec(
            num_scalar_prefetch=1,
            grid=(1,),
            in_specs=[full(N_CTX, KVH, SROWS, WID)] + [full(KVH, TOK, WID)] * 4 + [full(KVH, WID, WID)],
            out_specs=[full(KVH, TOK, WID)] * 2,
        ),
        out_shape=[shape(KVH, TOK, WID)] * 2,
        compiler_params=params(),
        name="later",
    )(docs, all_states, gkf, gv, kf, values, key_map)
    back = lambda x: jnp.transpose(x, (1, 0, 2))[None]
    return (back(gq), back(grad_keys), back(grad_values), maps[:, :rows].reshape(mq.shape), maps[:, rows:].reshape(mk.shape))


def solution(mesh):
    torus = Mesh(
        mesh.devices.reshape(mesh.shape["dp"], 4, 4, mesh.shape["head"]),
        ("dp", "ctx_0", "ctx_1", "head"),
    )
    rows = P("dp", CTX, "head", None)
    placed = (rows, rows, rows, P("head", None, None), P("head", None, None), P("dp", None))
    return jax.shard_map(
        body, mesh=torus, in_specs=placed, out_specs=(rows, rows, rows, placed[3], placed[4]), check_vma=False
    )
```
